128 devices in a mesh: lat: 8 (over z_lo, y), lon: 16 (over z_hi, x, core).
Axes of the slice: x: 4, y: 4, z: 4 (z_hi: 2, z_lo: 2; z = z_hi * 2 + z_lo), core: 2. Of those that a mesh axis runs over, the one named last changes fastest.
Arguments:
- control: float32 [96, 128, 4096], P(None, 'lat', 'lon'), may hold values from -6 to 6
- winds: float32 [4, 2, 128, 4096], P(None, None, 'lat', 'lon'), may hold values from -0.45 to 0.45
- pattern: int32 [128, 32, 13], P('lat', 'lon'), may hold values 0 or 1
- cov_tables: bfloat16 [7, 128, 128], replicated, may hold values from -0.21875 to 0.21875
- jacobians: bfloat16 [128, 128, 32, 96], P(('lat', 'lon')), may hold values from -1.25 to 1.25
- obs_value: bfloat16 [128, 128, 32], P(('lat', 'lon')), may hold values from -6 to 6
- obs_weight: bfloat16 [128, 128, 32], P(('lat', 'lon')), may hold values from 0.25 to 4
- obs_column: int32 [128, 128, 32], P(('lat', 'lon')), may hold values from 0 to 4095
- obs_count: int32 [128, 128], P(('lat', 'lon')), may hold values from 0 to 32, as said below
Outputs:
- forecast_increment: float32 [96, 128, 4096], P(None, 'lat', 'lon')
- gradient: float32 [96, 128, 4096], P(None, 'lat', 'lon')
The draws below stay inside these ranges and needn't reach their ends.
Inputs may be any that keep to these rules, and one draw needn't show every extreme that they name: The first obs_count[src, dst] slots from src to patch dst are live; every draw has a patch that receives 32 live slots from every source device.
All inputs are finite; a program needn't handle non-finite values. No bound on the sum of `pattern` on one device may be relied on, other than what follows from the above.
Results may differ from the reference program's by a relative error of at most 0.0029.
Values may be sent and summed in bfloat16 or wider, within the bound.
A program may use at most 64 MiB of HBM per device.

```python
import math
import jax
import jax.numpy as jnp

BLOCK = 128
R = 6
STEPS = 4
CLAT = 16
CAP = 32
CHANNEL_COUNT = 96
OFFS = 13
CLON = 256
LATITUDE_ROWS = 128
LONGITUDE_COLUMNS = 4096
NBLOCKS = 32
N_LAT = 8
N_LON = 16
DEVICES = 128


def draw_obs_count(key, part):
    key_base = jax.random.fold_in(key, 11)
    key_heavy = jax.random.fold_in(key, 12)
    key_pick = jax.random.fold_in(key, 13)
    base_counts = jax.random.randint(key_base, (DEVICES, DEVICES), 0, CAP // 2 + 1)
    heavy_dest = jax.random.randint(key_heavy, (DEVICES,), 0, 4) == 0
    chosen = jax.random.randint(key_pick, (), 0, DEVICES)
    heavy_dest = heavy_dest | (jnp.arange(DEVICES) == chosen)
    return jnp.where(heavy_dest[None, :], CAP, base_counts).astype(jnp.int32)


def set_ends(drawn, stream_key, least, top_value):
    longest = drawn.shape.index(max(drawn.shape))
    spots = []
    for shift in (0, 1):
        where = [jax.random.randint(jax.random.fold_in(stream_key, axis), (), 0, length) for axis, length in enumerate(drawn.shape)]
        where[longest] = (where[longest] + shift) % drawn.shape[longest]
        spots.append(tuple(where))
    return drawn.at[spots[0]].set(least).at[spots[1]].set(top_value)


def shard_levels(stream_key, shape, split, smallest, largest):
    def one(position, parts):
        heights = jax.random.uniform(jax.random.fold_in(jax.random.fold_in(stream_key, 6), position), (parts,), jnp.float32, smallest / len(split), largest / len(split))
        return jnp.repeat(jnp.exp(heights), shape[position] // parts).reshape((-1,) + (1,) * (len(shape) - position - 1))

    loudness = one(*split[0])
    for cut in split[1:]:
        loudness = loudness * one(*cut)
    return loudness


def scatter_about(own_key, extent, spread, limit, split=(), held_as=jnp.bfloat16):
    factor_of = shard_levels(own_key, extent, split, -0.22, 0.18) if split else 1.0
    values = jax.random.normal(own_key, extent, jnp.float32) * spread * factor_of
    return jnp.minimum(jnp.maximum(values, -limit), limit).astype(held_as)


def setup_inputs(seed: int = 0) -> dict:
    keys = jax.random.split(jax.random.key(seed), 10)
    return {
        "control": scatter_about(keys[0], (CHANNEL_COUNT, LATITUDE_ROWS, LONGITUDE_COLUMNS), 1.0, 6.0, ((1, 8), (2, 16)), jnp.float32),
        "winds": jnp.clip(jax.random.uniform(keys[1], (STEPS, 2, LATITUDE_ROWS, LONGITUDE_COLUMNS), jnp.float32, -0.45, 0.45) * shard_levels(keys[1], (STEPS, 2, LATITUDE_ROWS, LONGITUDE_COLUMNS), ((2, 8), (3, 16)), -0.4, 0.0), -0.45, 0.45),
        "pattern": set_ends((jax.random.randint(keys[2], (LATITUDE_ROWS, NBLOCKS, OFFS), 0, 2) < 1).astype(jnp.int32), jax.random.fold_in(keys[2], 1), 0, 1),
        "cov_tables": scatter_about(keys[3], (R + 1, BLOCK, BLOCK), (BLOCK * R) ** -0.5, 0.21875),
        "jacobians": scatter_about(keys[4], (N_LAT * N_LON, N_LAT * N_LON, CAP, CHANNEL_COUNT), (CHANNEL_COUNT // 4) ** -0.5, 1.25, ((0, 128),)),
        "obs_value": scatter_about(keys[5], (N_LAT * N_LON, N_LAT * N_LON, CAP), 1.0, 6.0, ((0, 128),)),
        "obs_weight": jnp.clip(jnp.exp(math.log(4.0) - 2.7725887 * jax.random.uniform(keys[6], (N_LAT * N_LON, N_LAT * N_LON, CAP), jnp.float32) ** shard_levels(keys[6], (N_LAT * N_LON, N_LAT * N_LON, CAP), ((0, 128),), -0.2, 0.2)), 0.25, 4.0).astype(jnp.bfloat16),
        "obs_column": set_ends(jax.random.randint(keys[7], (N_LAT * N_LON, N_LAT * N_LON, CAP), 0, CLAT * CLON), jax.random.fold_in(keys[7], 1), 0, (CLAT * CLON) - 1).astype(jnp.int32),
        "obs_count": draw_obs_count(jax.random.fold_in(keys[9], 71), 0),
    }


def wind_factors(wind):
    zonal = wind[0]
    meridional = wind[1]
    abs_zonal = jnp.abs(zonal)
    abs_merid = jnp.abs(meridional)
    return (1.0 - abs_zonal - abs_merid, 0.5 * (abs_zonal - zonal), 0.5 * (abs_zonal + zonal),
            0.5 * (abs_merid - meridional), 0.5 * (abs_merid + meridional))


def row_next(field):
    return jnp.concatenate([field[:, 1:, :], jnp.zeros_like(field[:, :1, :])], axis=1)


def row_prev(field):
    return jnp.concatenate([jnp.zeros_like(field[:, :1, :]), field[:, :-1, :]], axis=1)


def forward_advect(field, factors):
    w_centre, w_east, w_west, w_north, w_south = factors
    return (w_centre * field + w_east * jnp.roll(field, -1, 2) + w_west * jnp.roll(field, 1, 2)
            + w_north * row_next(field) + w_south * row_prev(field))


def adjoint_advect(field, factors):
    w_centre, w_east, w_west, w_north, w_south = factors
    return (w_centre * field + jnp.roll(w_east * field, 1, 2) + jnp.roll(w_west * field, -1, 2)
            + row_prev(w_north * field) + row_next(w_south * field))


def reference(control, winds, pattern, cov_tables, jacobians, obs_value, obs_weight, obs_column, obs_count):
    nblk = LONGITUDE_COLUMNS // BLOCK
    control_b = control.astype(jnp.bfloat16)
    padded = jnp.pad(control_b, ((0, 0), (R, R), (0, 0)))
    increment = jnp.zeros((CHANNEL_COUNT, LATITUDE_ROWS, nblk, BLOCK), jnp.float32)
    for offset in range(-R, R + 1):
        block_rows = padded[:, R + offset:R + offset + LATITUDE_ROWS, :].reshape(CHANNEL_COUNT, LATITUDE_ROWS, nblk, BLOCK)
        term = jnp.einsum('cibk,kl->cibl', block_rows.astype(jnp.float32), cov_tables[abs(offset)].astype(jnp.float32))
        increment = increment + term * pattern[:, :, offset + R].astype(jnp.float32)[None, :, :, None]
    present_state = increment.reshape(CHANNEL_COUNT, LATITUDE_ROWS, LONGITUDE_COLUMNS)
    for step in range(STEPS):
        present_state = forward_advect(present_state, wind_factors(winds[step]))
    predicted_state = present_state

    dest = jnp.broadcast_to(jnp.arange(DEVICES, dtype=jnp.int32)[None, :, None], obs_column.shape)
    glob_row = (dest // N_LON) * CLAT + obs_column // CLON
    glob_col = (dest % N_LON) * CLON + obs_column % CLON
    indices = (glob_row * LONGITUDE_COLUMNS + glob_col).reshape(-1)
    flattened_state = predicted_state.reshape(CHANNEL_COUNT, LATITUDE_ROWS * LONGITUDE_COLUMNS)
    gathered = flattened_state[:, indices]
    jac_rows = jacobians.reshape(-1, CHANNEL_COUNT).astype(jnp.float32).T
    evolved = jnp.sum(jac_rows * gathered, axis=0)
    alive_slots = (jnp.arange(CAP, dtype=jnp.int32)[None, None, :] < obs_count[:, :, None]).reshape(-1)
    residual = jnp.where(alive_slots, obs_weight.reshape(-1).astype(jnp.float32)
                         * (evolved - obs_value.reshape(-1).astype(jnp.float32)), jnp.float32(0.0))
    forcing = jnp.zeros_like(flattened_state).at[:, indices].add(jac_rows * residual[None, :])
    adjoint = forcing.reshape(CHANNEL_COUNT, LATITUDE_ROWS, LONGITUDE_COLUMNS)
    for step in range(STEPS - 1, -1, -1):
        adjoint = adjoint_advect(adjoint, wind_factors(winds[step]))

    adjoint_b = adjoint.astype(jnp.bfloat16)
    padded_adj = jnp.pad(adjoint_b, ((0, 0), (R, R), (0, 0)))
    padded_pat = jnp.pad(pattern, ((R, R), (0, 0), (0, 0)))
    back = jnp.zeros((CHANNEL_COUNT, LATITUDE_ROWS, nblk, BLOCK), jnp.float32)
    for offset in range(-R, R + 1):
        block_rows = padded_adj[:, R - offset:R - offset + LATITUDE_ROWS, :].reshape(CHANNEL_COUNT, LATITUDE_ROWS, nblk, BLOCK)
        mask_rows = padded_pat[R - offset:R - offset + LATITUDE_ROWS, :, offset + R].astype(jnp.float32)
        term = jnp.einsum('cibl,kl->cibk', block_rows.astype(jnp.float32), cov_tables[abs(offset)].astype(jnp.float32))
        back = back + term * mask_rows[None, :, :, None]
    gradient = control + back.reshape(CHANNEL_COUNT, LATITUDE_ROWS, LONGITUDE_COLUMNS)
    return predicted_state, gradient
```

```python
import functools

import jax
import jax.numpy as jnp
from jax import lax
from jax.experimental import pallas as pl
from jax.experimental.pallas import tpu as pltpu
from jax.sharding import PartitionSpec as P

BLOCK = 128
R = 6
OFFS = 2 * R + 1
STEPS = 4
H = STEPS
ROWS = 16
COLS = 256
CH = 96
EXT = ROWS + 2 * H
WIDE = ROWS + 2 * R
RING = COLS + 128
LANES = 128
CHUNK = 16
F32 = jnp.float32
BF16 = jnp.bfloat16
MESH = pl.DeviceIdType.MESH
NORTH, SOUTH, EAST, WEST = 0, 1, 2, 3


def neighbours():
    n_lat = lax.axis_size("lat")
    n_lon = lax.axis_size("lon")
    p = lax.axis_index("lat")
    q = lax.axis_index("lon")
    return (
        (lax.rem(p + 1, n_lat), q),
        (lax.rem(p + n_lat - 1, n_lat), q),
        (p, lax.rem(q + 1, n_lon)),
        (p, lax.rem(q + n_lon - 1, n_lon)),
    )


def greet():
    barrier = pltpu.get_barrier_semaphore()
    for who in neighbours():
        pl.semaphore_signal(barrier, inc=1, device_id=who, device_id_type=MESH)
    pl.semaphore_wait(barrier, 4)


def send(src, dst, sems, index, side):
    copy = pltpu.make_async_remote_copy(
        src_ref=src,
        dst_ref=dst,
        send_sem=sems.at[0, index],
        recv_sem=sems.at[1, index],
        device_id=neighbours()[side],
        device_id_type=MESH,
    )
    copy.start()
    return copy


def lane_iota(shape):
    return lax.broadcasted_iota(jnp.int32, shape, 1)


def pack_strip(read, east):
    total = None
    for rr in range(EXT):
        tile = read(rr)
        lanes = lane_iota(tile.shape)
        shift = (H * rr - (LANES - H if east else 0)) % LANES
        moved = tile if shift == 0 else pltpu.roll(tile, shift, 1)
        here = (lanes >= H * rr) & (lanes < H * rr + H)
        total = jnp.where(here, moved, 0.0 if total is None else total)
    return total


def unpack_strips(from_west, from_east, rr):
    lanes = lane_iota(from_west.shape)
    west_shift = (LANES - H - H * rr) % LANES
    east_shift = (LANES - H * rr) % LANES
    west = from_west if west_shift == 0 else pltpu.roll(from_west, west_shift, 1)
    east = from_east if east_shift == 0 else pltpu.roll(from_east, east_shift, 1)
    return jnp.where(lanes < H, east, jnp.where(lanes >= LANES - H, west, 0.0))


def row_valid(rr):
    n_lat = lax.axis_size("lat")
    row = lax.axis_index("lat") * ROWS + rr - H
    return jnp.where((row >= 0) & (row < ROWS * n_lat), 1.0, 0.0).astype(F32)


def wind_rows(wext, rr, step):
    zonal = wext[rr, 2 * step : 2 * step + 1, :]
    merid = wext[rr, 2 * step + 1 : 2 * step + 2, :]
    return zonal, merid, jnp.abs(zonal), jnp.abs(merid), row_valid(rr)


def spread(w):
    return jnp.broadcast_to(w, (CHUNK, RING))


def forward_row(src, wext, rr, step, emit):
    zonal, merid, az, am, valid = wind_rows(wext, rr, step)
    half = 0.5 * valid
    wc = spread((1.0 - az - am) * valid)
    we = spread(half * (az - zonal))
    ww = spread(half * (az + zonal))
    wn = spread(half * (am - merid))
    ws = spread(half * (am + merid))
    for c in range(0, CH, CHUNK):
        here = src[rr, c : c + CHUNK, :]
        value = (
            wc * here
            + we * pltpu.roll(here, RING - 1, 1)
            + ww * pltpu.roll(here, 1, 1)
            + wn * src[rr + 1, c : c + CHUNK, :]
            + ws * src[rr - 1, c : c + CHUNK, :]
        )
        emit(c, value)


def adjoint_row(src, wext, rr, step, emit):
    zonal, merid, az, am, valid = wind_rows(wext, rr, step)
    half = 0.5 * valid
    wc = spread((1.0 - az - am) * valid)
    we = spread(half * (az - zonal))
    ww = spread(half * (az + zonal))
    _, merid, _, am, valid = wind_rows(wext, rr - 1, step)
    wn = spread(0.5 * valid * (am - merid))
    _, merid, _, am, valid = wind_rows(wext, rr + 1, step)
    ws = spread(0.5 * valid * (am + merid))
    for c in range(0, CH, CHUNK):
        here = src[rr, c : c + CHUNK, :]
        value = (
            wc * here
            + pltpu.roll(we * here, 1, 1)
            + pltpu.roll(ww * here, RING - 1, 1)
            + wn * src[rr - 1, c : c + CHUNK, :]
            + ws * src[rr + 1, c : c + CHUNK, :]
        )
        emit(c, value)


def advance(row, src, dst, wext, step, margin):
    def body(rr, carry):
        def emit(c, value):
            dst[rr, c : c + CHUNK, :] = value

        row(src, wext, rr, step, emit)
        return carry

    lax.fori_loop(margin, EXT - margin, body, 0)


def cov_pair(base, ext, pat, lhs, cov, adjoint):
    for n in range(2):
        for b in range(2):
            m = (2 * n + b) * CH
            for k in range(OFFS):
                at = base + n + (2 * R - k if adjoint else k)
                at_pat = at if adjoint else base + n
                mask = pat[at_pat, 16 * b + k : 16 * b + k + 1, :]
                mask = jnp.broadcast_to(mask, (16, BLOCK)).astype(BF16)
                rows = ext[at, :, b * BLOCK : (b + 1) * BLOCK].reshape(CH // 16, 16, BLOCK)
                lhs[m : m + CH, k * BLOCK : (k + 1) * BLOCK] = (rows * mask[None]).reshape(CH, BLOCK)
    return jnp.dot(lhs[...], cov[...], preferred_element_type=F32)


def pair_base(t):
    return jnp.where(t < 2, 6 + 2 * t, jnp.where(t < 5, 2 * t - 4, 2 * t))


def halves(hbm, local, sems, inward):
    copies = []
    for h in range(2):
        far = hbm.at[:, pl.ds(h * LANES, LANES)]
        near = local.at[h]
        pair = (far, near) if inward else (near, far)
        copies.append(pltpu.make_async_copy(*pair, sems.at[h]))
    for copy in copies:
        copy.start()
    return copies


def exchange_rows(field, stage, sems, index):
    stage[0] = field[ROWS : ROWS + H, :, 0:COLS].astype(BF16)
    up = send(stage.at[0], stage.at[2], sems, index, NORTH)
    stage[1] = field[H : 2 * H, :, 0:COLS].astype(BF16)
    down = send(stage.at[1], stage.at[3], sems, index + 1, SOUTH)
    return up, down


def place_rows(field, stage):
    field[0:H, :, 0:COLS] = stage[2].astype(F32) * row_valid(0)
    field[ROWS + H : EXT, :, 0:COLS] = stage[3].astype(F32) * row_valid(EXT - 1)


def forward_kernel(
    ctrl, winds, pattern, cov, out, f2, wout, pout,
    ext, pext, pf, lhs, covcat, xa, xb, stage, wext, strips, grid, wgrid, sems, local,
):
    incoming = halves(ctrl, grid, local.at[0], True) + halves(winds, wgrid, local.at[1], True)
    greet()
    for copy in incoming:
        copy.wait()
    for r in range(ROWS):
        for h in range(2):
            lanes = slice(h * LANES, (h + 1) * LANES)
            ext[R + r, :, lanes] = grid[h, pl.ds(r, CH, stride=ROWS), :].astype(BF16)
            wext[H + r, :, lanes] = wgrid[h, pl.ds(r, 8, stride=ROWS), :]
        pext[R + r] = pattern[r]
    up = send(ext.at[pl.ds(ROWS, R)], ext.at[pl.ds(0, R)], sems, 0, NORTH)
    down = send(ext.at[pl.ds(R, R)], ext.at[pl.ds(R + ROWS, R)], sems, 1, SOUTH)
    w_up = send(
        wext.at[pl.ds(ROWS, H), :, pl.ds(0, COLS)], wext.at[pl.ds(0, H), :, pl.ds(0, COLS)],
        sems, 2, NORTH,
    )
    w_down = send(
        wext.at[pl.ds(H, H), :, pl.ds(0, COLS)], wext.at[pl.ds(ROWS + H, H), :, pl.ds(0, COLS)],
        sems, 3, SOUTH,
    )
    for k in range(OFFS):
        covcat[k * BLOCK : (k + 1) * BLOCK, :] = cov[abs(k - R)]
    pf[...] = pattern[...].astype(F32)

    def pair(t, carry):
        base = pair_base(t)
        y = cov_pair(base, ext, pf, lhs, covcat, False)
        for n in range(2):
            for b in range(2):
                m = (2 * n + b) * CH
                xa[H + base + n, :, b * BLOCK : (b + 1) * BLOCK] = y[m : m + CH]
        return carry

    lax.fori_loop(0, 2, pair, 0)
    up.wait()
    down.wait()
    lax.fori_loop(2, 8, pair, 0)
    x_up, x_down = exchange_rows(xa, stage, sems, 4)
    p_up = send(pext.at[pl.ds(ROWS, R)], pext.at[pl.ds(0, R)], sems, 6, NORTH)
    p_down = send(pext.at[pl.ds(R, R)], pext.at[pl.ds(R + ROWS, R)], sems, 7, SOUTH)
    w_up.wait()
    w_down.wait()
    x_up.wait()
    x_down.wait()
    place_rows(xa, stage)
    strips[0, 0:CH] = pack_strip(lambda rr: xa[rr, :, COLS - LANES : COLS], True)
    strips[0, CH : CH + 8] = pack_strip(lambda rr: wext[rr, :, COLS - LANES : COLS], True)
    east = send(strips.at[0], strips.at[2], sems, 8, EAST)
    strips[1, 0:CH] = pack_strip(lambda rr: xa[rr, :, 0:LANES], False)
    strips[1, CH : CH + 8] = pack_strip(lambda rr: wext[rr, :, 0:LANES], False)
    west = send(strips.at[1], strips.at[3], sems, 9, WEST)
    east.wait()
    west.wait()
    for rr in range(EXT):
        xa[rr, :, COLS:RING] = unpack_strips(strips[2, 0:CH], strips[3, 0:CH], rr)
        wext[rr, :, COLS:RING] = unpack_strips(
            strips[2, CH : CH + 8], strips[3, CH : CH + 8], rr
        )
    src, dst = xa, xb
    for step in range(STEPS - 1):
        advance(forward_row, src, dst, wext, step, step + 1)
        src, dst = dst, src

    def last(rr, carry):
        r = rr - H
        at = pl.multiple_of(r * COLS, COLS)

        def emit(c, value):
            value = value[:, 0:COLS]
            for h in range(2):
                lanes = slice(h * LANES, (h + 1) * LANES)
                grid[h, pl.ds(r + c * ROWS, CHUNK, stride=ROWS), :] = value[:, lanes]
            high = value.astype(BF16)
            f2[c : c + CHUNK, pl.ds(at, COLS)] = high
            f2[CH + c : CH + c + CHUNK, pl.ds(at, COLS)] = (value - high.astype(F32)).astype(BF16)

        forward_row(src, wext, rr, STEPS - 1, emit)
        return carry

    lax.fori_loop(H, H + ROWS, last, 0)
    outgoing = halves(out, grid, local.at[2], False)
    wout[...] = wext[...]
    p_up.wait()
    p_down.wait()
    pout[...] = pext[...]
    for copy in outgoing:
        copy.wait()


def adjoint_kernel(
    forcing, winds, pattern, cov, ctrl, out,
    ext, pf, lhs, covcat, xa, xb, stage, strips, grid, sems, local,
):
    incoming = halves(ctrl, grid, local.at[0], True)
    xa[H : H + ROWS, :, 0:COLS] = forcing[...]
    greet()
    up, down = exchange_rows(xa, stage, sems, 0)
    for k in range(R + 1):
        turned = cov[k].astype(F32).T.astype(BF16)
        for at in {R + k, R - k}:
            covcat[at * BLOCK : (at + 1) * BLOCK, :] = turned
    pf[...] = pattern[...].astype(F32)
    up.wait()
    down.wait()
    place_rows(xa, stage)
    strips[0] = pack_strip(lambda rr: xa[rr, :, COLS - LANES : COLS], True)
    east = send(strips.at[0], strips.at[2], sems, 2, EAST)
    strips[1] = pack_strip(lambda rr: xa[rr, :, 0:LANES], False)
    west = send(strips.at[1], strips.at[3], sems, 3, WEST)
    east.wait()
    west.wait()
    for rr in range(EXT):
        xa[rr, :, COLS:RING] = unpack_strips(strips[2], strips[3], rr)
    src, dst = xa, xb
    for n in range(STEPS - 1):
        advance(adjoint_row, src, dst, winds, STEPS - 1 - n, n + 1)
        src, dst = dst, src

    def last(rr, carry):
        def emit(c, value):
            ext[rr - H + R, c : c + CHUNK, :] = value[:, 0:COLS].astype(BF16)

        adjoint_row(src, winds, rr, 0, emit)
        return carry

    lax.fori_loop(H, H + ROWS, last, 0)
    up = send(ext.at[pl.ds(ROWS, R)], ext.at[pl.ds(0, R)], sems, 4, NORTH)
    down = send(ext.at[pl.ds(R, R)], ext.at[pl.ds(R + ROWS, R)], sems, 5, SOUTH)

    def pair(t, carry):
        base = pair_base(t)
        y = cov_pair(base, ext, pf, lhs, covcat, True)
        for n in range(2):
            for b in range(2):
                m = (2 * n + b) * CH
                rows = pl.ds(base + n, CH, stride=ROWS)
                grid[b, rows, :] = grid[b, rows, :] + y[m : m + CH]
        return carry

    for copy in incoming:
        copy.wait()
    lax.fori_loop(0, 2, pair, 0)
    up.wait()
    down.wait()
    lax.fori_loop(2, 8, pair, 0)
    for copy in halves(out, grid, local.at[1], False):
        copy.wait()


SLOTS = 4096
TILE = 256


def obs_kernel(rec, f2, out, r32, aux, ct, rowb, oh, y2):
    per = 32

    def widen(t, carry):
        at = pl.multiple_of(t * 512, 512)
        r32[pl.ds(at, 512), :] = rec[pl.ds(at, 512), :].astype(F32)
        return carry

    lax.fori_loop(0, SLOTS // 512, widen, 0)
    group = lane_iota((per, LANES)) // per
    for k in range(4):
        total = jnp.zeros((per, LANES), F32)
        for q in range(4):
            part = r32[pl.ds(q * per + k, per, stride=4 * per), :]
            total = jnp.where(group == q, pltpu.roll(part, (per * q + per) % LANES, 1), total)
        aux[k] = total
    sub = lax.broadcasted_iota(jnp.int32, (COLS, TILE), 0).astype(F32)

    def vector(k, t):
        return jnp.concatenate([aux[k, pl.ds(2 * t, 1), :], aux[k, pl.ds(2 * t + 1, 1), :]], axis=1)

    def gather(t, carry):
        at = pl.multiple_of(t * TILE, TILE)
        value, weight, row, col = (vector(k, t) for k in range(4))
        hot = jnp.where(jnp.broadcast_to(col, (COLS, TILE)) == sub, 1.0, 0.0).astype(BF16)
        ct[:, pl.ds(at, TILE)] = hot
        row16 = jnp.broadcast_to(row, (16, TILE))
        rowb[:, pl.ds(at, TILE)] = row16.astype(BF16)
        hot3 = hot.reshape(COLS // 16, 16, TILE)
        for r in range(ROWS):
            here = jnp.where(row16 == float(r), 1.0, 0.0).astype(BF16)
            oh[r * COLS : (r + 1) * COLS, 0:TILE] = (hot3 * here[None]).reshape(COLS, TILE)
        got = jnp.dot(f2[...], oh[...], preferred_element_type=F32)
        jac = jnp.concatenate(
            [r32[pl.ds(at, LANES), :].T[0:CH], r32[pl.ds(at + LANES, LANES), :].T[0:CH]], axis=1
        )
        evolved = jnp.sum(jac * (got[0:CH] + got[CH : 2 * CH]), axis=0, keepdims=True)
        residual = weight * (evolved - value)
        push = jac * residual
        high = push.astype(BF16)
        y2[0:CH, pl.ds(at, TILE)] = high
        y2[CH : 2 * CH, pl.ds(at, TILE)] = (push - high.astype(F32)).astype(BF16)
        return carry

    lax.fori_loop(0, SLOTS // TILE, gather, 0)

    def scatter(r, carry):
        want = r.astype(F32).astype(BF16)
        for c in range(0, SLOTS, 512):
            here = jnp.where(rowb[:, c : c + 512].astype(F32) == want.astype(F32), 1.0, 0.0).astype(BF16)
            part = ct[:, c : c + 512].reshape(COLS // 16, 16, 512) * here[None]
            oh2 = part.reshape(COLS, 512)
            term = lax.dot_general(
                y2[:, c : c + 512], oh2, (((1,), (1,)), ((), ())), preferred_element_type=F32
            )
            total = term if c == 0 else total + term
        out[r] = total[0:CH] + total[CH : 2 * CH]
        return carry

    lax.fori_loop(0, ROWS, scatter, 0)


def vmem(n):
    return [pl.BlockSpec(memory_space=pltpu.VMEM)] * n


def anywhere(n):
    return [pl.BlockSpec(memory_space=pl.ANY)] * n


def params(**more):
    return pltpu.CompilerParams(vmem_limit_bytes=60 * 1024 * 1024, **more)


def forward_call(ctrl, winds, pattern, cov):
    return pl.pallas_call(
        forward_kernel,
        name="forward",
        out_shape=(
            jax.ShapeDtypeStruct((CH * ROWS, COLS), F32),
            jax.ShapeDtypeStruct((2 * CH, ROWS * COLS), BF16),
            jax.ShapeDtypeStruct((EXT, 8, RING), F32),
            jax.ShapeDtypeStruct((WIDE, 32, BLOCK), BF16),
        ),
        in_specs=anywhere(2) + vmem(2),
        out_specs=tuple(anywhere(1) + vmem(3)),
        scratch_shapes=[
            pltpu.VMEM((WIDE, CH, COLS), BF16),
            pltpu.VMEM((WIDE, 32, BLOCK), BF16),
            pltpu.VMEM((ROWS, 32, BLOCK), F32),
            pltpu.VMEM((4 * CH, OFFS * BLOCK), BF16),
            pltpu.VMEM((OFFS * BLOCK, BLOCK), BF16),
            pltpu.VMEM((EXT, CH, RING), F32),
            pltpu.VMEM((EXT, CH, RING), F32),
            pltpu.VMEM((4, H, CH, COLS), BF16),
            pltpu.VMEM((EXT, 8, RING), F32),
            pltpu.VMEM((4, CH + 8, LANES), F32),
            pltpu.VMEM((2, CH * ROWS, LANES), F32),
            pltpu.VMEM((2, 2 * STEPS * ROWS, LANES), F32),
            pltpu.SemaphoreType.DMA((2, 10)),
            pltpu.SemaphoreType.DMA((3, 2)),
        ],
        compiler_params=params(collective_id=0, has_side_effects=True),
        cost_estimate=pl.CostEstimate(
            flops=3_000_000_000, bytes_accessed=16_000_000, transcendentals=0
        ),
    )(ctrl, winds, pattern, cov)


def adjoint_call(forcing, winds, pattern, cov, ctrl):
    return pl.pallas_call(
        adjoint_kernel,
        name="adjoint",
        out_shape=jax.ShapeDtypeStruct((CH * ROWS, COLS), F32),
        in_specs=vmem(4) + anywhere(1),
        out_specs=anywhere(1)[0],
        scratch_shapes=[
            pltpu.VMEM((WIDE, CH, COLS), BF16),
            pltpu.VMEM((WIDE, 32, BLOCK), F32),
            pltpu.VMEM((4 * CH, OFFS * BLOCK), BF16),
            pltpu.VMEM((OFFS * BLOCK, BLOCK), BF16),
            pltpu.VMEM((EXT, CH, RING), F32),
            pltpu.VMEM((EXT, CH, RING), F32),
            pltpu.VMEM((4, H, CH, COLS), BF16),
            pltpu.VMEM((4, CH, LANES), F32),
            pltpu.VMEM((2, CH * ROWS, LANES), F32),
            pltpu.SemaphoreType.DMA((2, 6)),
            pltpu.SemaphoreType.DMA((2, 2)),
        ],
        compiler_params=params(collective_id=1, has_side_effects=True),
    )(forcing, winds, pattern, cov, ctrl)


def obs_call(rec, f2):
    return pl.pallas_call(
        obs_kernel,
        name="observe",
        out_shape=jax.ShapeDtypeStruct((ROWS, CH, COLS), F32),
        in_specs=vmem(2),
        out_specs=vmem(1)[0],
        scratch_shapes=[
            pltpu.VMEM((SLOTS, LANES), F32),
            pltpu.VMEM((4, 32, LANES), F32),
            pltpu.VMEM((COLS, SLOTS), BF16),
            pltpu.VMEM((16, SLOTS), BF16),
            pltpu.VMEM((ROWS * COLS, TILE), BF16),
            pltpu.VMEM((2 * CH, SLOTS), BF16),
        ],
        compiler_params=params(),
    )(rec, f2)


def on_device(
    control, winds, pattern, cov_tables, jacobians, obs_value, obs_weight, obs_column, obs_count
):
    slots = obs_column.shape[2]
    live = lax.broadcasted_iota(jnp.int32, obs_column.shape[1:], 1) < obs_count[0][:, None]
    weight = jnp.where(live, obs_weight[0], jnp.zeros((), BF16))
    row = (obs_column[0] // COLS).astype(BF16)
    col = (obs_column[0] % COLS).astype(BF16)
    extra = jnp.stack([obs_value[0], weight, row, col], axis=1)
    extra = jnp.pad(extra, ((0, 0), (0, slots - 4), (0, 0)))
    record = jnp.concatenate([jacobians[0], extra], axis=2)
    rec = lax.all_to_all(record, ("lat", "lon"), split_axis=0, concat_axis=0, tiled=True)

    rows_global = lax.axis_index("lat") * ROWS + jnp.arange(ROWS, dtype=jnp.int32)
    reached = rows_global[:, None] + jnp.arange(-R, R + 1, dtype=jnp.int32)[None, :]
    inside = (reached >= 0) & (reached < ROWS * lax.axis_size("lat"))
    mask = jnp.where(inside[:, None, :], pattern, 0)
    mask = jnp.pad(mask, ((0, 0), (0, 0), (0, 16 - OFFS))).reshape(ROWS, 32)
    mask = jnp.broadcast_to(mask.astype(BF16)[:, :, None], (ROWS, 32, BLOCK))

    ctrl = control.reshape(CH * ROWS, COLS)
    wind2 = winds.reshape(2 * STEPS * ROWS, COLS)
    forecast, f2, wext, pext = forward_call(ctrl, wind2, mask, cov_tables)
    forcing = obs_call(rec.reshape(SLOTS, LANES), f2)
    gradient = adjoint_call(forcing, wext, pext, cov_tables, ctrl)
    return forecast.reshape(CH, ROWS, COLS), gradient.reshape(CH, ROWS, COLS)


def solution(mesh):
    in_specs = (
        P(None, "lat", "lon"),
        P(None, None, "lat", "lon"),
        P("lat", "lon", None),
        P(),
        P(("lat", "lon"), None, None, None),
        P(("lat", "lon"), None, None),
        P(("lat", "lon"), None, None),
        P(("lat", "lon"), None, None),
        P(("lat", "lon"), None),
    )
    out_specs = (P(None, "lat", "lon"), P(None, "lat", "lon"))
    return jax.shard_map(
        on_device, mesh=mesh, in_specs=in_specs, out_specs=out_specs, check_vma=False
    )
```

```python
import jax
import jax.numpy as jnp
from jax import lax
from jax.experimental import pallas as pl
from jax.experimental.pallas import tpu as pltpu
from jax.sharding import PartitionSpec as P

BLOCK = 128
R = 6
OFFS = 2 * R + 1
STEPS = 4
H = STEPS
ROWS = 16
COLS = 256
CH = 96
EXT = ROWS + 2 * H
WIDE = ROWS + 2 * R
RING = COLS + 128
LANES = 128
SLOTS = 4096
TILE = 256
GROUP = 4
F32 = jnp.float32
BF16 = jnp.bfloat16
MESH = pl.DeviceIdType.MESH
NORTH, SOUTH, EAST, WEST = 0, 1, 2, 3


def neighbours():
    n_lat = lax.axis_size("lat")
    n_lon = lax.axis_size("lon")
    p = lax.axis_index("lat")
    q = lax.axis_index("lon")
    return (
        (lax.rem(p + 1, n_lat), q),
        (lax.rem(p + n_lat - 1, n_lat), q),
        (p, lax.rem(q + 1, n_lon)),
        (p, lax.rem(q + n_lon - 1, n_lon)),
    )


def greet():
    barrier = pltpu.get_barrier_semaphore()
    for who in neighbours():
        pl.semaphore_signal(barrier, inc=1, device_id=who, device_id_type=MESH)
    pl.semaphore_wait(barrier, 4)


def send(src, dst, sems, index, side):
    copy = pltpu.make_async_remote_copy(
        src_ref=src,
        dst_ref=dst,
        send_sem=sems.at[0, index],
        recv_sem=sems.at[1, index],
        device_id=neighbours()[side],
        device_id_type=MESH,
    )
    copy.start()
    return copy


def wait(copies):
    for copy in copies:
        copy.wait()


def lane_iota(shape):
    return lax.broadcasted_iota(jnp.int32, shape, 1)


def turn(x, shift):
    shift %= LANES
    return x if shift == 0 else pltpu.roll(x, shift, 1)


def pack_strip(read, first):
    total = None
    for r in range(ROWS):
        tile = read(r + H)
        at = H * (r + H)
        lanes = lane_iota(tile.shape)
        moved = turn(tile, at - first)
        total = jnp.where((lanes >= at) & (lanes < at + H), moved, 0.0 if total is None else total)
    return total


def halo_tile(west, west_at, east, east_at):
    lanes = lane_iota(west.shape)
    west = turn(west, LANES - H - west_at)
    east = turn(east, -east_at)
    return jnp.where(lanes < H, east, jnp.where(lanes >= LANES - H, west, 0.0))


def corners(west, east):
    lanes = lane_iota(west.shape)
    width = H * H
    top, low = H * ROWS, H * H
    of_west = ((lanes >= top) & (lanes < top + width)) | ((lanes >= low) & (lanes < low + width))
    return jnp.where(of_west, west, turn(east, width))


def own_halo(strips, a, b, rr):
    return halo_tile(strips[2, a:b], H * rr, strips[3, a:b], H * rr)


def corner_halo(strips, a, b, rr):
    slot, at = (5, H * (rr + ROWS)) if rr < H else (6, H * (rr - ROWS))
    slab = strips[slot, a:b]
    return halo_tile(slab, at, slab, at + H * H)


def row_valid(rr):
    n_lat = lax.axis_size("lat")
    row = lax.axis_index("lat") * ROWS + rr - H
    return jnp.where((row >= 0) & (row < ROWS * n_lat), 1.0, 0.0).astype(F32)


def wind_rows(wext, rr, step):
    zonal = wext[rr, 2 * step : 2 * step + 1, :]
    merid = wext[rr, 2 * step + 1 : 2 * step + 2, :]
    return zonal, merid, jnp.abs(zonal), jnp.abs(merid)


def spread(w):
    return jnp.broadcast_to(w, (8, RING))


def forward_row(src, wext, rr, step, emit):
    zonal, merid, az, am = wind_rows(wext, rr, step)
    valid = row_valid(rr)
    wc = spread((1.0 - az - am) * valid)
    wz = spread(az * valid)
    wm = spread(am * valid)
    from_east = spread(zonal) < 0
    from_north = spread(merid) < 0

    def part(c):
        here = src[rr, c : c + 8, :]
        along = jnp.where(from_east, pltpu.roll(here, RING - 1, 1), pltpu.roll(here, 1, 1))
        across = jnp.where(from_north, src[rr + 1, c : c + 8, :], src[rr - 1, c : c + 8, :])
        return wc * here + wz * along + wm * across

    for c in range(0, CH, 16):
        emit(c, part(c), part(c + 8))


def adjoint_row(src, wext, rr, step, emit):
    zonal, _, az, am = wind_rows(wext, rr, step)
    half = 0.5 * row_valid(rr)
    wc = spread((1.0 - az - am) * row_valid(rr))
    we = pltpu.roll(spread(half * (az - zonal)), 1, 1)
    ww = pltpu.roll(spread(half * (az + zonal)), RING - 1, 1)
    _, merid, _, am = wind_rows(wext, rr - 1, step)
    wn = spread(0.5 * row_valid(rr - 1) * (am - merid))
    _, merid, _, am = wind_rows(wext, rr + 1, step)
    ws = spread(0.5 * row_valid(rr + 1) * (am + merid))

    def part(c):
        here = src[rr, c : c + 8, :]
        return (
            wc * here
            + we * pltpu.roll(here, 1, 1)
            + ww * pltpu.roll(here, RING - 1, 1)
            + wn * src[rr - 1, c : c + 8, :]
            + ws * src[rr + 1, c : c + 8, :]
        )

    for c in range(0, CH, 16):
        emit(c, part(c), part(c + 8))


def advance(row, src, dst, wext, step, pairs, base, emit=None):
    def store(rr):
        def put(c, low, high):
            dst[rr, c : c + 8, :] = low
            dst[rr, c + 8 : c + 16, :] = high

        return put

    def body(t, carry):
        for k in range(2):
            rr = base(t) + k
            row(src, wext, rr, step, (emit or store)(rr))
        return carry

    lax.fori_loop(0, pairs, body, 0)


def inner(row, xa, xb, wext, steps, emit):
    src, dst = xa, xb
    for n in range(STEPS):
        first = H + 1 + n
        last = emit if n == STEPS - 1 else None
        advance(row, src, dst, wext, steps[n], 7 - n, lambda t, first=first: first + 2 * t, last)
        src, dst = dst, src


def outer(row, xa, xb, wext, steps, emit):
    src, dst = xa, xb
    for n in range(STEPS):
        low, high = 1 + n, H + ROWS - 1 - n
        last = emit if n == STEPS - 1 else None
        advance(
            row, src, dst, wext, steps[n], 4,
            lambda t, low=low, high=high: 2 * t + jnp.where(t < 2, low, high - 4), last,
        )
        src, dst = dst, src


def cov_pair(base, ext, pat, lhs, cov, adjoint):
    for n in range(2):
        for b in range(2):
            m = (2 * n + b) * CH
            for k in range(OFFS):
                at = base + n + (2 * R - k if adjoint else k)
                at_pat = at if adjoint else base + n
                mask = pat[at_pat, 16 * b + k : 16 * b + k + 1, :]
                mask = jnp.broadcast_to(mask, (16, BLOCK)).astype(BF16)
                rows = ext[at, :, b * BLOCK : (b + 1) * BLOCK].reshape(CH // 16, 16, BLOCK)
                lhs[m : m + CH, k * BLOCK : (k + 1) * BLOCK] = (rows * mask[None]).reshape(CH, BLOCK)
    return jnp.dot(lhs[...], cov[...], preferred_element_type=F32)


def send_pair(ext, sems, index, up, down):
    return (
        send(ext.at[pl.ds(R + up, 2)], ext.at[pl.ds(R + up - ROWS, 2)], sems, index, NORTH),
        send(ext.at[pl.ds(R + down, 2)], ext.at[pl.ds(R + down + ROWS, 2)], sems, index + 1, SOUTH),
    )


def send_rows(field, stage, sems, index, up, down, count, at):
    here = pl.ds(at, count)
    stage[0, at : at + count] = field[H + up : H + up + count, :, 0:COLS].astype(BF16)
    north = send(stage.at[0, here], stage.at[2, here], sems, index, NORTH)
    stage[1, at : at + count] = field[H + down : H + down + count, :, 0:COLS].astype(BF16)
    south = send(stage.at[1, here], stage.at[3, here], sems, index + 1, SOUTH)
    return north, south


def place_rows(field, stage, north_order, south_order):
    low, high = row_valid(0), row_valid(EXT - 1)
    for k in range(H):
        field[k, :, 0:COLS] = stage[2, north_order[k]].astype(F32) * low
        field[ROWS + H + k, :, 0:COLS] = stage[3, south_order[k]].astype(F32) * high


def send_strips(strips, sems, index, put):
    put(0, COLS - LANES, LANES - H)
    east = send(strips.at[0], strips.at[2], sems, index, EAST)
    put(1, 0, 0)
    west = send(strips.at[1], strips.at[3], sems, index + 1, WEST)
    return east, west


def send_corners(strips, sems, index):
    strips[4] = corners(strips[2], strips[3])
    return (
        send(strips.at[4], strips.at[5], sems, index, NORTH),
        send(strips.at[4], strips.at[6], sems, index + 1, SOUTH),
    )


def forward_kernel(
    ctrl, winds, pattern, cov, fin, wout, pout,
    raw, ext, pext, pf, lhs, covcat, xa, xb, stage, wext, strips, sems, local,
):
    order = (14, 15, 0, 1, 12, 13, 2, 3, 10, 11, 4, 5, 6, 7, 8, 9)
    rows_in = {r: pltpu.make_async_copy(ctrl.at[:, r, :], raw.at[r], local.at[0, r]) for r in order}
    winds_in = [
        pltpu.make_async_copy(winds.at[:, r, :], wext.at[H + r, :, pl.ds(0, COLS)], local.at[1, r])
        for r in range(ROWS)
    ]
    for r in order:
        rows_in[r].start()
    for copy in winds_in:
        copy.start()
    greet()
    chunks = []
    for n, (up, down) in enumerate(((14, 0), (12, 2), (10, 4))):
        for r in (up, up + 1, down, down + 1):
            rows_in[r].wait()
            ext[R + r] = raw[r].astype(BF16)
        chunks.append(send_pair(ext, sems, 2 * n, up, down))
    wait(winds_in)
    wide = pl.ds(0, COLS)
    wind_rows_sent = (
        send(wext.at[pl.ds(ROWS, H), :, wide], wext.at[pl.ds(0, H), :, wide], sems, 6, NORTH),
        send(wext.at[pl.ds(H, H), :, wide], wext.at[pl.ds(ROWS + H, H), :, wide], sems, 7, SOUTH),
    )
    for r in range(6, 10):
        rows_in[r].wait()
        ext[R + r] = raw[r].astype(BF16)
    for k in range(OFFS):
        covcat[k * BLOCK : (k + 1) * BLOCK, :] = cov[abs(k - R)]
    pf[...] = pattern[...].astype(F32)
    for r in range(ROWS):
        pext[R + r] = pattern[r]

    def pairs(first, gap):
        def pair(t, carry):
            base = first + gap * t
            y = cov_pair(base, ext, pf, lhs, covcat, False)
            for n in range(2):
                for b in range(2):
                    m = (2 * n + b) * CH
                    xa[H + base + n, :, b * BLOCK : (b + 1) * BLOCK] = y[m : m + CH]
            return carry

        lax.fori_loop(0, 2, pair, 0)

    pairs(6, 2)
    wait(chunks[0])
    pairs(4, 6)
    wait(chunks[1])
    pairs(2, 10)
    near = send_rows(xa, stage, sems, 8, 12, 2, 2, 0)
    wait(chunks[2])
    pairs(0, 14)
    far = send_rows(xa, stage, sems, 10, 14, 0, 2, 2)

    def put(slot, at, first):
        strips[slot, 0:CH] = pack_strip(lambda rr: xa[rr, :, at : at + LANES], first)
        strips[slot, CH : CH + 8] = pack_strip(lambda rr: wext[rr, :, at : at + LANES], first)

    wait(send_strips(strips, sems, 12, put))
    turned = send_corners(strips, sems, 14)
    patterns = [
        send(pext.at[pl.ds(ROWS, R)], pext.at[pl.ds(0, R)], sems, 16, NORTH),
        send(pext.at[pl.ds(R, R)], pext.at[pl.ds(R + ROWS, R)], sems, 17, SOUTH),
    ]
    for rr in range(H, H + ROWS):
        xa[rr, :, COLS:RING] = own_halo(strips, 0, CH, rr)
        wext[rr, :, COLS:RING] = own_halo(strips, CH, CH + 8, rr)

    def emit(rr):
        def put(c, low, high):
            fin[rr - H, c : c + 8, :] = low[:, 0:COLS]
            fin[rr - H, c + 8 : c + 16, :] = high[:, 0:COLS]

        return put

    steps = tuple(range(STEPS))
    inner(forward_row, xa, xb, wext, steps, emit)
    wait(near + far + turned + wind_rows_sent)
    place_rows(xa, stage, (0, 1, 2, 3), (2, 3, 0, 1))
    for rr in (*range(H), *range(H + ROWS, EXT)):
        xa[rr, :, COLS:RING] = corner_halo(strips, 0, CH, rr) * row_valid(rr)
        wext[rr, :, COLS:RING] = corner_halo(strips, CH, CH + 8, rr)
    outer(forward_row, xa, xb, wext, steps, emit)
    wout[...] = wext[...]
    wait(patterns)
    pout[...] = pext[...]


def adjoint_kernel(
    forcing, winds, pattern, cov, out,
    ext, pf, lhs, covcat, xa, xb, stage, strips, back, sems, local,
):
    greet()
    xa[H : H + ROWS, :, 0:COLS] = forcing[...]
    rows = send_rows(xa, stage, sems, 0, 12, 0, 4, 0)

    def put(slot, at, first):
        strips[slot] = pack_strip(lambda rr: xa[rr, :, at : at + LANES], first)

    sides = send_strips(strips, sems, 2, put)
    for k in range(R + 1):
        turned = cov[k].astype(F32).T.astype(BF16)
        for at in {R + k, R - k}:
            covcat[at * BLOCK : (at + 1) * BLOCK, :] = turned
    pf[...] = pattern[...].astype(F32)
    wait(sides)
    turned = send_corners(strips, sems, 4)
    for rr in range(H, H + ROWS):
        xa[rr, :, COLS:RING] = own_halo(strips, 0, CH, rr)

    def emit(rr):
        def put(c, low, high):
            both = jnp.concatenate([low[:, 0:COLS], high[:, 0:COLS]], axis=0)
            ext[rr - H + R, c : c + 16, :] = both.astype(BF16)

        return put

    steps = tuple(range(STEPS - 1, -1, -1))
    inner(adjoint_row, xa, xb, winds, steps, emit)
    chunks = [send_pair(ext, sems, 6, 10, 4)]
    wait(rows + turned)
    place_rows(xa, stage, (0, 1, 2, 3), (0, 1, 2, 3))
    for rr in (*range(H), *range(H + ROWS, EXT)):
        xa[rr, :, COLS:RING] = corner_halo(strips, 0, CH, rr)
    outer(adjoint_row, xa, xb, winds, steps, emit)
    chunks.append(send_pair(ext, sems, 8, 14, 0))
    chunks.append(send_pair(ext, sems, 10, 12, 2))
    outgoing = []

    def pairs(first, gap):
        def pair(t, carry):
            base = first + gap * t
            y = cov_pair(base, ext, pf, lhs, covcat, True)
            for n in range(2):
                for b in range(2):
                    m = (2 * n + b) * CH
                    back[base + n, :, b * BLOCK : (b + 1) * BLOCK] = y[m : m + CH]
            return carry

        lax.fori_loop(0, 2, pair, 0)
        for r in (first, first + 1, first + gap, first + gap + 1):
            copy = pltpu.make_async_copy(back.at[r], out.at[:, r, :], local.at[r])
            copy.start()
            outgoing.append(copy)

    pairs(6, 2)
    wait(chunks[1])
    pairs(4, 6)
    wait(chunks[2])
    pairs(2, 10)
    wait(chunks[0])
    pairs(0, 14)
    wait(outgoing)


def obs_kernel(rec, fin, forcing, forecast, field, f2, r32, aux, ct, rowb, yt, zt, local):
    per = 32
    field_in = pltpu.make_async_copy(fin, field, local.at[ROWS])
    field_in.start()

    def widen(t, carry):
        at = pl.multiple_of(t * 512, 512)
        r32[pl.ds(at, 512), :] = rec[pl.ds(at, 512), :].astype(F32)
        return carry

    lax.fori_loop(0, SLOTS // 512, widen, 0)
    group = lane_iota((per, LANES)) // per
    for k in range(4):
        total = jnp.zeros((per, LANES), F32)
        for q in range(4):
            part = r32[pl.ds(q * per + k, per, stride=4 * per), :]
            total = jnp.where(group == q, turn(part, per * q + per), total)
        aux[k] = total
    field_in.wait()
    outgoing = []
    for r in range(ROWS):
        copy = pltpu.make_async_copy(field.at[r], forecast.at[:, r, :], local.at[r])
        copy.start()
        outgoing.append(copy)
    for r in range(ROWS):
        high = field[r].astype(BF16)
        f2[0, r * CH : (r + 1) * CH, :] = high
        f2[1, r * CH : (r + 1) * CH, :] = (field[r] - high.astype(F32)).astype(BF16)
    sub = lax.broadcasted_iota(jnp.int32, (COLS, TILE), 0).astype(F32)

    def vector(k, t):
        return jnp.concatenate([aux[k, pl.ds(2 * t, 1), :], aux[k, pl.ds(2 * t + 1, 1), :]], axis=1)

    def gather(t, carry):
        at = pl.multiple_of(t * TILE, TILE)
        value, weight, row, col = (vector(k, t) for k in range(4))
        hot = jnp.where(jnp.broadcast_to(col, (COLS, TILE)) == sub, 1.0, 0.0).astype(BF16)
        ct[:, pl.ds(at, TILE)] = hot
        row8 = jnp.broadcast_to(row, (8, TILE))
        rowb[:, pl.ds(at, TILE)] = jnp.broadcast_to(row, (16, TILE)).astype(BF16)
        halves = []
        for part in range(2):
            got = jnp.zeros((CH // 8, 8, TILE), F32)
            for g in range(0, ROWS, GROUP):
                rows = f2[part, g * CH : (g + GROUP) * CH, :]
                some = jnp.dot(rows, hot, preferred_element_type=F32)
                for k in range(GROUP):
                    piece = some[k * CH : (k + 1) * CH].reshape(CH // 8, 8, TILE)
                    got = jnp.where((row8 == float(g + k))[None], piece, got)
            halves.append(got)
        got = (halves[0] + halves[1]).reshape(CH, TILE)
        jac = jnp.concatenate(
            [r32[pl.ds(at, LANES), :].T[0:CH], r32[pl.ds(at + LANES, LANES), :].T[0:CH]], axis=1
        )
        evolved = jnp.sum(jac * got, axis=0, keepdims=True)
        residual = weight * (evolved - value)
        yt[:, pl.ds(at, TILE)] = (jac * residual).astype(BF16)
        return carry

    lax.fori_loop(0, SLOTS // TILE, gather, 0)

    def scatter(g, carry):
        for k in range(GROUP):
            want = (g * GROUP + k).astype(F32)
            for c in range(0, SLOTS, 512):
                here = jnp.where(rowb[:, c : c + 512].astype(F32) == want, 1.0, 0.0).astype(BF16)
                part = yt[:, c : c + 512].reshape(CH // 16, 16, 512) * here[None]
                zt[k * CH : (k + 1) * CH, c : c + 512] = part.reshape(CH, 512)
        total = lax.dot_general(
            zt[...], ct[...], (((1,), (1,)), ((), ())), preferred_element_type=F32
        )
        for k in range(GROUP):
            forcing[g * GROUP + k] = total[k * CH : (k + 1) * CH]
        return carry

    lax.fori_loop(0, ROWS // GROUP, scatter, 0)
    wait(outgoing)


def vmem(n):
    return [pl.BlockSpec(memory_space=pltpu.VMEM)] * n


def anywhere(n):
    return [pl.BlockSpec(memory_space=pl.ANY)] * n


def params(**more):
    return pltpu.CompilerParams(vmem_limit_bytes=60 * 1024 * 1024, **more)


def advection_scratch(strip_rows):
    return [
        pltpu.VMEM((EXT, CH, RING), F32),
        pltpu.VMEM((EXT, CH, RING), F32),
        pltpu.VMEM((4, H, CH, COLS), BF16),
        pltpu.VMEM((7, strip_rows, LANES), F32),
    ]


def covariance_scratch(pattern_rows):
    return [
        pltpu.VMEM((pattern_rows, 32, BLOCK), F32),
        pltpu.VMEM((4 * CH, OFFS * BLOCK), BF16),
        pltpu.VMEM((OFFS * BLOCK, BLOCK), BF16),
    ]


def forward_call(ctrl, winds, pattern, cov):
    xa, xb, stage, strips = advection_scratch(CH + 8)
    return pl.pallas_call(
        forward_kernel,
        name="forward",
        out_shape=(
            jax.ShapeDtypeStruct((ROWS, CH, COLS), F32),
            jax.ShapeDtypeStruct((EXT, 8, RING), F32),
            jax.ShapeDtypeStruct((WIDE, 32, BLOCK), BF16),
        ),
        in_specs=anywhere(2) + vmem(2),
        out_specs=tuple(vmem(3)),
        scratch_shapes=[
            pltpu.VMEM((ROWS, CH, COLS), F32),
            pltpu.VMEM((WIDE, CH, COLS), BF16),
            pltpu.VMEM((WIDE, 32, BLOCK), BF16),
            *covariance_scratch(ROWS),
            xa,
            xb,
            stage,
            pltpu.VMEM((EXT, 8, RING), F32),
            strips,
            pltpu.SemaphoreType.DMA((2, 18)),
            pltpu.SemaphoreType.DMA((2, ROWS)),
        ],
        compiler_params=params(collective_id=0, has_side_effects=True),
        cost_estimate=pl.CostEstimate(
            flops=3_000_000_000, bytes_accessed=16_000_000, transcendentals=0
        ),
    )(ctrl, winds, pattern, cov)


def adjoint_call(forcing, winds, pattern, cov):
    xa, xb, stage, strips = advection_scratch(CH)
    return pl.pallas_call(
        adjoint_kernel,
        name="adjoint",
        out_shape=jax.ShapeDtypeStruct((CH, ROWS, COLS), F32),
        in_specs=vmem(4),
        out_specs=anywhere(1)[0],
        scratch_shapes=[
            pltpu.VMEM((WIDE, CH, COLS), BF16),
            *covariance_scratch(WIDE),
            xa,
            xb,
            stage,
            strips,
            pltpu.VMEM((ROWS, CH, COLS), F32),
            pltpu.SemaphoreType.DMA((2, 12)),
            pltpu.SemaphoreType.DMA((ROWS,)),
        ],
        compiler_params=params(collective_id=1, has_side_effects=True),
    )(forcing, winds, pattern, cov)


def obs_call(rec, fin):
    return pl.pallas_call(
        obs_kernel,
        name="observe",
        out_shape=(
            jax.ShapeDtypeStruct((ROWS, CH, COLS), F32),
            jax.ShapeDtypeStruct((CH, ROWS, COLS), F32),
        ),
        in_specs=vmem(1) + anywhere(1),
        out_specs=tuple(vmem(1) + anywhere(1)),
        scratch_shapes=[
            pltpu.VMEM((ROWS, CH, COLS), F32),
            pltpu.VMEM((2, ROWS * CH, COLS), BF16),
            pltpu.VMEM((SLOTS, LANES), F32),
            pltpu.VMEM((4, 32, LANES), F32),
            pltpu.VMEM((COLS, SLOTS), BF16),
            pltpu.VMEM((16, SLOTS), BF16),
            pltpu.VMEM((CH, SLOTS), BF16),
            pltpu.VMEM((GROUP * CH, SLOTS), BF16),
            pltpu.SemaphoreType.DMA((ROWS + 1,)),
        ],
        compiler_params=params(),
    )(rec, fin)


def on_device(
    control, winds, pattern, cov_tables, jacobians, obs_value, obs_weight, obs_column, obs_count
):
    slots = obs_column.shape[2]
    live = lax.broadcasted_iota(jnp.int32, obs_column.shape[1:], 1) < obs_count[0][:, None]
    weight = jnp.where(live, obs_weight[0], jnp.zeros((), BF16))
    row = (obs_column[0] // COLS).astype(BF16)
    col = (obs_column[0] % COLS).astype(BF16)
    extra = jnp.stack([obs_value[0], weight, row, col], axis=1)
    extra = jnp.pad(extra, ((0, 0), (0, slots - 4), (0, 0)))
    record = jnp.concatenate([jacobians[0], extra], axis=2)
    rec = lax.all_to_all(record, ("lat", "lon"), split_axis=0, concat_axis=0, tiled=True)

    rows_global = lax.axis_index("lat") * ROWS + jnp.arange(ROWS, dtype=jnp.int32)
    reached = rows_global[:, None] + jnp.arange(-R, R + 1, dtype=jnp.int32)[None, :]
    inside = (reached >= 0) & (reached < ROWS * lax.axis_size("lat"))
    mask = jnp.where(inside[:, None, :], pattern, 0)
    mask = jnp.pad(mask, ((0, 0), (0, 0), (0, 16 - OFFS))).reshape(ROWS, 32)
    mask = jnp.broadcast_to(mask.astype(BF16)[:, :, None], (ROWS, 32, BLOCK))

    wind2 = winds.reshape(2 * STEPS, ROWS, COLS)
    fin, wext, pext = forward_call(control, wind2, mask, cov_tables)
    forcing, forecast = obs_call(rec.reshape(SLOTS, LANES), fin)
    back = adjoint_call(forcing, wext, pext, cov_tables)
    return forecast, control + back


def solution(mesh):
    in_specs = (
        P(None, "lat", "lon"),
        P(None, None, "lat", "lon"),
        P("lat", "lon", None),
        P(),
        P(("lat", "lon"), None, None, None),
        P(("lat", "lon"), None, None),
        P(("lat", "lon"), None, None),
        P(("lat", "lon"), None, None),
        P(("lat", "lon"), None),
    )
    out_specs = (P(None, "lat", "lon"), P(None, "lat", "lon"))
    return jax.shard_map(
        on_device, mesh=mesh, in_specs=in_specs, out_specs=out_specs, check_vma=False
    )
```

```python
import jax
import jax.numpy as jnp
from jax import lax
from jax.experimental import pallas as pl
from jax.experimental.pallas import tpu as pltpu
from jax.sharding import PartitionSpec as P

BLOCK = 128
R = 6
OFFS = 2 * R + 1
STEPS = 4
H = STEPS
ROWS = 16
COLS = 256
CH = 96
EXT = ROWS + 2 * H
WIDE = ROWS + 2 * R
RING = COLS + 128
LANES = 128
SLOTS = 4096
TILE = 256
GROUP = 4
WAVE = 49
F32 = jnp.float32
BF16 = jnp.bfloat16
MESH = pl.DeviceIdType.MESH
NORTH, SOUTH, EAST, WEST = 0, 1, 2, 3


def neighbours():
    n_lat = lax.axis_size("lat")
    n_lon = lax.axis_size("lon")
    p = lax.axis_index("lat")
    q = lax.axis_index("lon")
    return (
        (lax.rem(p + 1, n_lat), q),
        (lax.rem(p + n_lat - 1, n_lat), q),
        (p, lax.rem(q + 1, n_lon)),
        (p, lax.rem(q + n_lon - 1, n_lon)),
    )


def nth_peer(k):
    n_lon = lax.axis_size("lon")
    n = lax.axis_size("lat") * n_lon
    other = lax.rem(lax.axis_index("lat") * n_lon + lax.axis_index("lon") + 45 * k, n)
    return other, (lax.div(other, n_lon), lax.rem(other, n_lon))


def greet_all():
    barrier = pltpu.get_barrier_semaphore()
    n = lax.axis_size("lat") * lax.axis_size("lon")

    def signal(k, carry):
        _, who = nth_peer(k)
        pl.semaphore_signal(barrier, inc=1, device_id=who, device_id_type=MESH)
        return carry

    lax.fori_loop(1, n, signal, 0)
    pl.semaphore_wait(barrier, n - 1)


def greet():
    barrier = pltpu.get_barrier_semaphore()
    for who in neighbours():
        pl.semaphore_signal(barrier, inc=1, device_id=who, device_id_type=MESH)
    pl.semaphore_wait(barrier, 4)


def send(src, dst, sems, index, side):
    copy = pltpu.make_async_remote_copy(
        src_ref=src,
        dst_ref=dst,
        send_sem=sems.at[0, index],
        recv_sem=sems.at[1, index],
        device_id=neighbours()[side],
        device_id_type=MESH,
    )
    copy.start()
    return copy


def wait(copies):
    for copy in copies:
        copy.wait()


def lane_iota(shape):
    return lax.broadcasted_iota(jnp.int32, shape, 1)


def turn(x, shift):
    shift %= LANES
    return x if shift == 0 else pltpu.roll(x, shift, 1)


def pack_strip(read, first):
    total = None
    for r in range(ROWS):
        tile = read(r + H)
        at = H * (r + H)
        lanes = lane_iota(tile.shape)
        moved = turn(tile, at - first)
        total = jnp.where((lanes >= at) & (lanes < at + H), moved, 0.0 if total is None else total)
    return total


def halo_tile(west, west_at, east, east_at):
    lanes = lane_iota(west.shape)
    west = turn(west, LANES - H - west_at)
    east = turn(east, -east_at)
    return jnp.where(lanes < H, east, jnp.where(lanes >= LANES - H, west, 0.0))


def corners(west, east):
    lanes = lane_iota(west.shape)
    width = H * H
    top, low = H * ROWS, H * H
    of_west = ((lanes >= top) & (lanes < top + width)) | ((lanes >= low) & (lanes < low + width))
    return jnp.where(of_west, west, turn(east, width))


def own_halo(strips, a, b, rr):
    return halo_tile(strips[2, a:b], H * rr, strips[3, a:b], H * rr)


def corner_halo(strips, a, b, rr):
    slot, at = (5, H * (rr + ROWS)) if rr < H else (6, H * (rr - ROWS))
    slab = strips[slot, a:b]
    return halo_tile(slab, at, slab, at + H * H)


def row_valid(rr):
    n_lat = lax.axis_size("lat")
    row = lax.axis_index("lat") * ROWS + rr - H
    return jnp.where((row >= 0) & (row < ROWS * n_lat), 1.0, 0.0).astype(F32)


def wind_rows(wext, rr, step):
    zonal = wext[rr, 2 * step : 2 * step + 1, :]
    merid = wext[rr, 2 * step + 1 : 2 * step + 2, :]
    return zonal, merid, jnp.abs(zonal), jnp.abs(merid)


def spread(w):
    return jnp.broadcast_to(w, (8, RING))


def forward_row(src, wext, rr, step, emit):
    zonal, merid, az, am = wind_rows(wext, rr, step)
    valid = row_valid(rr)
    wc = spread((1.0 - az - am) * valid)
    wz = spread(az * valid)
    wm = spread(am * valid)
    from_east = spread(zonal) < 0
    from_north = spread(merid) < 0

    def part(c):
        here = src[rr, c : c + 8, :]
        along = jnp.where(from_east, pltpu.roll(here, RING - 1, 1), pltpu.roll(here, 1, 1))
        across = jnp.where(from_north, src[rr + 1, c : c + 8, :], src[rr - 1, c : c + 8, :])
        return wc * here + wz * along + wm * across

    for c in range(0, CH, 16):
        emit(c, part(c), part(c + 8))


def adjoint_row(src, wext, rr, step, emit):
    zonal, _, az, am = wind_rows(wext, rr, step)
    half = 0.5 * row_valid(rr)
    wc = spread((1.0 - az - am) * row_valid(rr))
    we = pltpu.roll(spread(half * (az - zonal)), 1, 1)
    ww = pltpu.roll(spread(half * (az + zonal)), RING - 1, 1)
    _, merid, _, am = wind_rows(wext, rr - 1, step)
    wn = spread(0.5 * row_valid(rr - 1) * (am - merid))
    _, merid, _, am = wind_rows(wext, rr + 1, step)
    ws = spread(0.5 * row_valid(rr + 1) * (am + merid))

    def part(c):
        here = src[rr, c : c + 8, :]
        return (
            wc * here
            + we * pltpu.roll(here, 1, 1)
            + ww * pltpu.roll(here, RING - 1, 1)
            + wn * src[rr - 1, c : c + 8, :]
            + ws * src[rr + 1, c : c + 8, :]
        )

    for c in range(0, CH, 16):
        emit(c, part(c), part(c + 8))


def advance(row, src, dst, wext, step, pairs, base, emit=None):
    def store(rr):
        def put(c, low, high):
            dst[rr, c : c + 8, :] = low
            dst[rr, c + 8 : c + 16, :] = high

        return put

    def body(t, carry):
        for k in range(2):
            rr = base(t) + k
            row(src, wext, rr, step, (emit or store)(rr))
        return carry

    lax.fori_loop(0, pairs, body, 0)


def inner(row, xa, xb, wext, steps, emit):
    src, dst = xa, xb
    for n in range(STEPS):
        first = H + 1 + n
        last = emit if n == STEPS - 1 else None
        advance(row, src, dst, wext, steps[n], 7 - n, lambda t, first=first: first + 2 * t, last)
        src, dst = dst, src


def outer(row, xa, xb, wext, steps, emit):
    src, dst = xa, xb
    for n in range(STEPS):
        low, high = 1 + n, H + ROWS - 1 - n
        last = emit if n == STEPS - 1 else None
        advance(
            row, src, dst, wext, steps[n], 4,
            lambda t, low=low, high=high: 2 * t + jnp.where(t < 2, low, high - 4), last,
        )
        src, dst = dst, src


def cov_pair(base, ext, pat, lhs, cov, adjoint):
    for n in range(2):
        for b in range(2):
            m = (2 * n + b) * CH
            for k in range(OFFS):
                at = base + n + (2 * R - k if adjoint else k)
                at_pat = at if adjoint else base + n
                mask = pat[at_pat, 2 * k + b : 2 * k + b + 1, :]
                mask = jnp.broadcast_to(mask, (16, BLOCK)).astype(BF16)
                rows = ext[at, :, b * BLOCK : (b + 1) * BLOCK].reshape(CH // 16, 16, BLOCK)
                lhs[m : m + CH, k * BLOCK : (k + 1) * BLOCK] = (rows * mask[None]).reshape(CH, BLOCK)
    return jnp.dot(lhs[...], cov[...], preferred_element_type=F32)


def send_pair(ext, sems, index, up, down):
    return (
        send(ext.at[pl.ds(R + up, 2)], ext.at[pl.ds(R + up - ROWS, 2)], sems, index, NORTH),
        send(ext.at[pl.ds(R + down, 2)], ext.at[pl.ds(R + down + ROWS, 2)], sems, index + 1, SOUTH),
    )


def send_rows(field, stage, sems, index, up, down, count, at):
    here = pl.ds(at, count)
    stage[0, at : at + count] = field[H + up : H + up + count, :, 0:COLS].astype(BF16)
    north = send(stage.at[0, here], stage.at[2, here], sems, index, NORTH)
    stage[1, at : at + count] = field[H + down : H + down + count, :, 0:COLS].astype(BF16)
    south = send(stage.at[1, here], stage.at[3, here], sems, index + 1, SOUTH)
    return north, south


def place_rows(field, stage, north_order, south_order):
    low, high = row_valid(0), row_valid(EXT - 1)
    for k in range(H):
        field[k, :, 0:COLS] = stage[2, north_order[k]].astype(F32) * low
        field[ROWS + H + k, :, 0:COLS] = stage[3, south_order[k]].astype(F32) * high


def send_strips(strips, sems, index, put):
    put(0, COLS - LANES, LANES - H)
    east = send(strips.at[0], strips.at[2], sems, index, EAST)
    put(1, 0, 0)
    west = send(strips.at[1], strips.at[3], sems, index + 1, WEST)
    return east, west


def send_corners(strips, sems, index):
    strips[4] = corners(strips[2], strips[3])
    return (
        send(strips.at[4], strips.at[5], sems, index, NORTH),
        send(strips.at[4], strips.at[6], sems, index + 1, SOUTH),
    )


def pattern_table(pattern, table):
    table[...] = jnp.zeros_like(table)
    for k in range(OFFS):
        table[2 * k : 2 * k + 2, 0:ROWS] = pattern[k].astype(F32)
    shape = table.shape
    offset = lax.broadcasted_iota(jnp.int32, shape, 0) // 2 - R
    row = lax.axis_index("lat") * ROWS + lane_iota(shape) + offset
    inside = (row >= 0) & (row < ROWS * lax.axis_size("lat"))
    table[...] = jnp.where(inside, table[...], 0.0)


def records(jac, value, weight, column, count, wide, packed):
    slots = value.shape[0]
    live = lax.broadcasted_iota(jnp.int32, value.shape, 0) < jnp.broadcast_to(count[...], value.shape)
    cell = column[...]
    extra = (
        value[...].astype(F32),
        jnp.where(live, weight[...].astype(F32), 0.0),
        lax.shift_right_logical(cell, 8).astype(F32),
        jnp.bitwise_and(cell, COLS - 1).astype(F32),
    )

    def put(s, low):
        block = jnp.concatenate([jac[s].astype(F32), low], axis=0)
        wide[pl.ds(s, LANES, stride=slots), :] = block.T

    for s in range(4):
        put(s, extra[s])

    def rest(s, carry):
        put(s, jnp.zeros(value.shape, F32))
        return carry

    lax.fori_loop(4, slots, rest, 0)

    def narrow(t, carry):
        at = pl.multiple_of(t * 512, 512)
        packed[pl.ds(at, 512), :] = wide[pl.ds(at, 512), :].astype(BF16)
        return carry

    lax.fori_loop(0, SLOTS // 512, narrow, 0)


def record_copy(packed, rec, sems, k):
    per = SLOTS // (lax.axis_size("lat") * lax.axis_size("lon"))
    me = lax.axis_index("lat") * lax.axis_size("lon") + lax.axis_index("lon")
    other, who = nth_peer(k)
    return pltpu.make_async_remote_copy(
        src_ref=packed.at[pl.ds(pl.multiple_of(other * per, per), per)],
        dst_ref=rec.at[pl.ds(pl.multiple_of(me * per, per), per)],
        send_sem=sems.at[0, k],
        recv_sem=sems.at[1, k],
        device_id=who,
        device_id_type=MESH,
    )


def send_records(packed, rec, sems, first, last):
    def one(k, carry):
        record_copy(packed, rec, sems, k).start()
        return carry

    lax.fori_loop(first, last, one, 0)


def wait_records(packed, rec, sems):
    def one(k, carry):
        record_copy(packed, rec, sems, k).wait()
        return carry

    lax.fori_loop(1, lax.axis_size("lat") * lax.axis_size("lon"), one, 0)


def forward_kernel(
    ctrl, winds, pattern, cov, jac, value, weight, column, count, fin, wout, pout, rec,
    raw, ext, tables, pf, lhs, covcat, xa, xb, stage, wext, strips, wide_rec, packed, sems, local, rsems,
):
    order = (14, 15, 0, 1, 12, 13, 2, 3, 10, 11, 4, 5, 6, 7, 8, 9)
    rows_in = {r: pltpu.make_async_copy(ctrl.at[:, r, :], raw.at[r], local.at[0, r]) for r in order}
    winds_in = [
        pltpu.make_async_copy(winds.at[:, r, :], wext.at[H + r, :, pl.ds(0, COLS)], local.at[1, r])
        for r in range(ROWS)
    ]
    for r in order:
        rows_in[r].start()
    for copy in winds_in:
        copy.start()
    pattern_table(pattern, tables.at[0])
    greet_all()
    chunks = []
    for n, (up, down) in enumerate(((14, 0), (12, 2), (10, 4))):
        for r in (up, up + 1, down, down + 1):
            rows_in[r].wait()
            ext[R + r] = raw[r].astype(BF16)
        chunks.append(send_pair(ext, sems, 2 * n, up, down))
    wait(winds_in)
    wide = pl.ds(0, COLS)
    wind_rows_sent = (
        send(wext.at[pl.ds(ROWS, H), :, wide], wext.at[pl.ds(0, H), :, wide], sems, 6, NORTH),
        send(wext.at[pl.ds(H, H), :, wide], wext.at[pl.ds(ROWS + H, H), :, wide], sems, 7, SOUTH),
    )
    for r in range(6, 10):
        rows_in[r].wait()
        ext[R + r] = raw[r].astype(BF16)
    patterns = [
        send(tables.at[0], tables.at[1], sems, 16, NORTH),
        send(tables.at[0], tables.at[2], sems, 17, SOUTH),
    ]
    records(jac, value, weight, column, count, wide_rec, packed)
    peers = lax.axis_size("lat") * lax.axis_size("lon")
    per = SLOTS // peers
    me = lax.axis_index("lat") * lax.axis_size("lon") + lax.axis_index("lon")
    mine = pl.ds(pl.multiple_of(me * per, per), per)
    own = pltpu.make_async_copy(packed.at[mine], rec.at[mine], local.at[2, 0])
    own.start()
    send_records(packed, rec, rsems, 1, WAVE)
    for k in range(OFFS):
        covcat[k * BLOCK : (k + 1) * BLOCK, :] = cov[abs(k - R)]
    for r in range(ROWS):
        pf[r] = jnp.broadcast_to(tables[0, :, r : r + 1], (32, BLOCK))

    def pairs(first, gap):
        def pair(t, carry):
            base = first + gap * t
            y = cov_pair(base, ext, pf, lhs, covcat, False)
            for n in range(2):
                for b in range(2):
                    m = (2 * n + b) * CH
                    xa[H + base + n, :, b * BLOCK : (b + 1) * BLOCK] = y[m : m + CH]
            return carry

        lax.fori_loop(0, 2, pair, 0)

    pairs(6, 2)
    wait(chunks[0])
    pairs(4, 6)
    wait(chunks[1])
    pairs(2, 10)
    near = send_rows(xa, stage, sems, 8, 12, 2, 2, 0)
    wait(chunks[2])
    pairs(0, 14)
    far = send_rows(xa, stage, sems, 10, 14, 0, 2, 2)

    def put(slot, at, first):
        strips[slot, 0:CH] = pack_strip(lambda rr: xa[rr, :, at : at + LANES], first)
        strips[slot, CH : CH + 8] = pack_strip(lambda rr: wext[rr, :, at : at + LANES], first)

    wait(send_strips(strips, sems, 12, put))
    turned = send_corners(strips, sems, 14)
    send_records(packed, rec, rsems, WAVE, peers)
    for rr in range(H, H + ROWS):
        xa[rr, :, COLS:RING] = own_halo(strips, 0, CH, rr)
        wext[rr, :, COLS:RING] = own_halo(strips, CH, CH + 8, rr)

    def emit(rr):
        def put(c, low, high):
            fin[rr - H, c : c + 8, :] = low[:, 0:COLS]
            fin[rr - H, c + 8 : c + 16, :] = high[:, 0:COLS]

        return put

    steps = tuple(range(STEPS))
    inner(forward_row, xa, xb, wext, steps, emit)
    wait(near + far + turned + wind_rows_sent)
    place_rows(xa, stage, (0, 1, 2, 3), (2, 3, 0, 1))
    for rr in (*range(H), *range(H + ROWS, EXT)):
        xa[rr, :, COLS:RING] = corner_halo(strips, 0, CH, rr) * row_valid(rr)
        wext[rr, :, COLS:RING] = corner_halo(strips, CH, CH + 8, rr)
    outer(forward_row, xa, xb, wext, steps, emit)
    wout[...] = wext[...]
    wait(patterns)
    pout[...] = tables[...]
    own.wait()
    wait_records(packed, rec, rsems)


def adjoint_kernel(
    forcing, winds, pattern, cov, ctrl, out,
    ext, pf, lhs, covcat, xa, xb, stage, strips, back, sems, local,
):
    incoming = [
        pltpu.make_async_copy(ctrl.at[:, r, :], back.at[r], local.at[1, r]) for r in range(ROWS)
    ]
    for copy in incoming:
        copy.start()
    greet()
    xa[H : H + ROWS, :, 0:COLS] = forcing[...]
    rows = send_rows(xa, stage, sems, 0, 12, 0, 4, 0)

    def put(slot, at, first):
        strips[slot] = pack_strip(lambda rr: xa[rr, :, at : at + LANES], first)

    sides = send_strips(strips, sems, 2, put)
    for k in range(R + 1):
        turned = cov[k].astype(F32).T.astype(BF16)
        for at in {R + k, R - k}:
            covcat[at * BLOCK : (at + 1) * BLOCK, :] = turned
    for i in range(WIDE):
        r = i - R
        slot, lane = (1, r + ROWS) if r < 0 else (2, r - ROWS) if r >= ROWS else (0, r)
        pf[i] = jnp.broadcast_to(pattern[slot, :, lane : lane + 1], (32, BLOCK))
    wait(sides)
    turned = send_corners(strips, sems, 4)
    for rr in range(H, H + ROWS):
        xa[rr, :, COLS:RING] = own_halo(strips, 0, CH, rr)

    def emit(rr):
        def put(c, low, high):
            both = jnp.concatenate([low[:, 0:COLS], high[:, 0:COLS]], axis=0)
            ext[rr - H + R, c : c + 16, :] = both.astype(BF16)

        return put

    steps = tuple(range(STEPS - 1, -1, -1))
    inner(adjoint_row, xa, xb, winds, steps, emit)
    chunks = [send_pair(ext, sems, 6, 10, 4)]
    wait(rows + turned)
    place_rows(xa, stage, (0, 1, 2, 3), (0, 1, 2, 3))
    for rr in (*range(H), *range(H + ROWS, EXT)):
        xa[rr, :, COLS:RING] = corner_halo(strips, 0, CH, rr)
    outer(adjoint_row, xa, xb, winds, steps, emit)
    chunks.append(send_pair(ext, sems, 8, 14, 0))
    chunks.append(send_pair(ext, sems, 10, 12, 2))
    outgoing = []
    wait(incoming)

    def pairs(first, gap):
        def pair(t, carry):
            base = first + gap * t
            y = cov_pair(base, ext, pf, lhs, covcat, True)
            for n in range(2):
                for b in range(2):
                    m = (2 * n + b) * CH
                    lanes = slice(b * BLOCK, (b + 1) * BLOCK)
                    back[base + n, :, lanes] = back[base + n, :, lanes] + y[m : m + CH]
            return carry

        lax.fori_loop(0, 2, pair, 0)
        for r in (first, first + 1, first + gap, first + gap + 1):
            copy = pltpu.make_async_copy(back.at[r], out.at[:, r, :], local.at[0, r])
            copy.start()
            outgoing.append(copy)

    pairs(6, 2)
    wait(chunks[1])
    pairs(4, 6)
    wait(chunks[2])
    pairs(2, 10)
    wait(chunks[0])
    pairs(0, 14)
    wait(outgoing)


def obs_kernel(rec, fin, forcing, forecast, field, f2, r32, aux, ct, rowb, yt, zt, local):
    per = 32
    field_in = pltpu.make_async_copy(fin, field, local.at[ROWS])
    field_in.start()

    def widen(t, carry):
        at = pl.multiple_of(t * 512, 512)
        r32[pl.ds(at, 512), :] = rec[pl.ds(at, 512), :].astype(F32)
        return carry

    lax.fori_loop(0, SLOTS // 512, widen, 0)
    group = lane_iota((per, LANES)) // per
    for k in range(4):
        total = jnp.zeros((per, LANES), F32)
        for q in range(4):
            part = r32[pl.ds(q * per + k, per, stride=4 * per), :]
            total = jnp.where(group == q, turn(part, per * q + per), total)
        aux[k] = total
    field_in.wait()
    outgoing = []
    for r in range(ROWS):
        copy = pltpu.make_async_copy(field.at[r], forecast.at[:, r, :], local.at[r])
        copy.start()
        outgoing.append(copy)
    for r in range(ROWS):
        high = field[r].astype(BF16)
        f2[0, r * CH : (r + 1) * CH, :] = high
        f2[1, r * CH : (r + 1) * CH, :] = (field[r] - high.astype(F32)).astype(BF16)
    sub = lax.broadcasted_iota(jnp.int32, (COLS, TILE), 0).astype(F32)

    def vector(k, t):
        return jnp.concatenate([aux[k, pl.ds(2 * t, 1), :], aux[k, pl.ds(2 * t + 1, 1), :]], axis=1)

    def gather(t, carry):
        at = pl.multiple_of(t * TILE, TILE)
        value, weight, row, col = (vector(k, t) for k in range(4))
        hot = jnp.where(jnp.broadcast_to(col, (COLS, TILE)) == sub, 1.0, 0.0).astype(BF16)
        ct[:, pl.ds(at, TILE)] = hot
        row8 = jnp.broadcast_to(row, (8, TILE))
        rowb[:, pl.ds(at, TILE)] = jnp.broadcast_to(row, (16, TILE)).astype(BF16)
        halves = []
        for part in range(2):
            got = jnp.zeros((CH // 8, 8, TILE), F32)
            for g in range(0, ROWS, GROUP):
                rows = f2[part, g * CH : (g + GROUP) * CH, :]
                some = jnp.dot(rows, hot, preferred_element_type=F32)
                for k in range(GROUP):
                    piece = some[k * CH : (k + 1) * CH].reshape(CH // 8, 8, TILE)
                    got = jnp.where((row8 == float(g + k))[None], piece, got)
            halves.append(got)
        got = (halves[0] + halves[1]).reshape(CH, TILE)
        jac = jnp.concatenate(
            [r32[pl.ds(at, LANES), :].T[0:CH], r32[pl.ds(at + LANES, LANES), :].T[0:CH]], axis=1
        )
        evolved = jnp.sum(jac * got, axis=0, keepdims=True)
        residual = weight * (evolved - value)
        yt[:, pl.ds(at, TILE)] = (jac * residual).astype(BF16)
        return carry

    lax.fori_loop(0, SLOTS // TILE, gather, 0)

    def scatter(g, carry):
        for k in range(GROUP):
            want = (g * GROUP + k).astype(F32)
            for c in range(0, SLOTS, 512):
                here = jnp.where(rowb[:, c : c + 512].astype(F32) == want, 1.0, 0.0).astype(BF16)
                part = yt[:, c : c + 512].reshape(CH // 16, 16, 512) * here[None]
                zt[k * CH : (k + 1) * CH, c : c + 512] = part.reshape(CH, 512)
        total = lax.dot_general(
            zt[...], ct[...], (((1,), (1,)), ((), ())), preferred_element_type=F32
        )
        for k in range(GROUP):
            forcing[g * GROUP + k] = total[k * CH : (k + 1) * CH]
        return carry

    lax.fori_loop(0, ROWS // GROUP, scatter, 0)
    wait(outgoing)


def vmem(n):
    return [pl.BlockSpec(memory_space=pltpu.VMEM)] * n


def anywhere(n):
    return [pl.BlockSpec(memory_space=pl.ANY)] * n


def params(**more):
    return pltpu.CompilerParams(vmem_limit_bytes=60 * 1024 * 1024, **more)


def advection_scratch(strip_rows):
    return [
        pltpu.VMEM((EXT, CH, RING), F32),
        pltpu.VMEM((EXT, CH, RING), F32),
        pltpu.VMEM((4, H, CH, COLS), BF16),
        pltpu.VMEM((7, strip_rows, LANES), F32),
    ]


def covariance_scratch(pattern_rows):
    return [
        pltpu.VMEM((pattern_rows, 32, BLOCK), F32),
        pltpu.VMEM((4 * CH, OFFS * BLOCK), BF16),
        pltpu.VMEM((OFFS * BLOCK, BLOCK), BF16),
    ]


def forward_call(*args):
    xa, xb, stage, strips = advection_scratch(CH + 8)
    return pl.pallas_call(
        forward_kernel,
        name="forward",
        out_shape=(
            jax.ShapeDtypeStruct((ROWS, CH, COLS), F32),
            jax.ShapeDtypeStruct((EXT, 8, RING), F32),
            jax.ShapeDtypeStruct((3, 32, LANES), F32),
            jax.ShapeDtypeStruct((SLOTS, LANES), BF16),
        ),
        in_specs=anywhere(2) + vmem(7),
        out_specs=tuple(vmem(3) + anywhere(1)),
        scratch_shapes=[
            pltpu.VMEM((ROWS, CH, COLS), F32),
            pltpu.VMEM((WIDE, CH, COLS), BF16),
            pltpu.VMEM((3, 32, LANES), F32),
            *covariance_scratch(ROWS),
            xa,
            xb,
            stage,
            pltpu.VMEM((EXT, 8, RING), F32),
            strips,
            pltpu.VMEM((SLOTS, LANES), F32),
            pltpu.VMEM((SLOTS, LANES), BF16),
            pltpu.SemaphoreType.DMA((2, 18)),
            pltpu.SemaphoreType.DMA((3, ROWS)),
            pltpu.SemaphoreType.DMA((2, 128)),
        ],
        compiler_params=params(collective_id=0, has_side_effects=True),
        cost_estimate=pl.CostEstimate(
            flops=3_000_000_000, bytes_accessed=16_000_000, transcendentals=0
        ),
    )(*args)


def adjoint_call(forcing, winds, pattern, cov, ctrl):
    xa, xb, stage, strips = advection_scratch(CH)
    return pl.pallas_call(
        adjoint_kernel,
        name="adjoint",
        out_shape=jax.ShapeDtypeStruct((CH, ROWS, COLS), F32),
        in_specs=vmem(4) + anywhere(1),
        out_specs=anywhere(1)[0],
        scratch_shapes=[
            pltpu.VMEM((WIDE, CH, COLS), BF16),
            *covariance_scratch(WIDE),
            xa,
            xb,
            stage,
            strips,
            pltpu.VMEM((ROWS, CH, COLS), F32),
            pltpu.SemaphoreType.DMA((2, 12)),
            pltpu.SemaphoreType.DMA((2, ROWS)),
        ],
        compiler_params=params(collective_id=1, has_side_effects=True),
    )(forcing, winds, pattern, cov, ctrl)


def obs_call(rec, fin):
    return pl.pallas_call(
        obs_kernel,
        name="observe",
        out_shape=(
            jax.ShapeDtypeStruct((ROWS, CH, COLS), F32),
            jax.ShapeDtypeStruct((CH, ROWS, COLS), F32),
        ),
        in_specs=vmem(1) + anywhere(1),
        out_specs=tuple(vmem(1) + anywhere(1)),
        scratch_shapes=[
            pltpu.VMEM((ROWS, CH, COLS), F32),
            pltpu.VMEM((2, ROWS * CH, COLS), BF16),
            pltpu.VMEM((SLOTS, LANES), F32),
            pltpu.VMEM((4, 32, LANES), F32),
            pltpu.VMEM((COLS, SLOTS), BF16),
            pltpu.VMEM((16, SLOTS), BF16),
            pltpu.VMEM((CH, SLOTS), BF16),
            pltpu.VMEM((GROUP * CH, SLOTS), BF16),
            pltpu.SemaphoreType.DMA((ROWS + 1,)),
        ],
        compiler_params=params(),
    )(rec, fin)


def on_device(
    control, winds, pattern, cov_tables, jacobians, obs_value, obs_weight, obs_column, obs_count
):
    wind2 = winds.reshape(2 * STEPS, ROWS, COLS)
    fin, wext, table, rec = forward_call(
        control,
        wind2,
        jnp.transpose(pattern, (2, 1, 0)),
        cov_tables,
        jnp.transpose(jacobians[0], (1, 2, 0)),
        obs_value[0].T,
        obs_weight[0].T,
        obs_column[0].T,
        obs_count,
    )
    forcing, forecast = obs_call(rec, fin)
    gradient = adjoint_call(forcing, wext, table, cov_tables, control)
    return forecast, gradient


def solution(mesh):
    in_specs = (
        P(None, "lat", "lon"),
        P(None, None, "lat", "lon"),
        P("lat", "lon", None),
        P(),
        P(("lat", "lon"), None, None, None),
        P(("lat", "lon"), None, None),
        P(("lat", "lon"), None, None),
        P(("lat", "lon"), None, None),
        P(("lat", "lon"), None),
    )
    out_specs = (P(None, "lat", "lon"), P(None, "lat", "lon"))
    return jax.shard_map(
        on_device, mesh=mesh, in_specs=in_specs, out_specs=out_specs, check_vma=False
    )
```

```python
import jax
import jax.numpy as jnp
from jax import lax
from jax.experimental import pallas as pl
from jax.experimental.pallas import tpu as pltpu
from jax.sharding import PartitionSpec as P

BLOCK = 128
R = 6
OFFS = 2 * R + 1
STEPS = 4
H = STEPS
ROWS = 16
COLS = 256
CH = 96
EXT = ROWS + 2 * H
WIDE = ROWS + 2 * R
RING = COLS + 128
LANES = 128
SLOTS = 4096
TILE = 256
GROUP = 4
WAVE = 49
F32 = jnp.float32
BF16 = jnp.bfloat16
MESH = pl.DeviceIdType.MESH
NORTH, SOUTH, EAST, WEST = 0, 1, 2, 3


def neighbours():
    n_lat = lax.axis_size("lat")
    n_lon = lax.axis_size("lon")
    p = lax.axis_index("lat")
    q = lax.axis_index("lon")
    return (
        (lax.rem(p + 1, n_lat), q),
        (lax.rem(p + n_lat - 1, n_lat), q),
        (p, lax.rem(q + 1, n_lon)),
        (p, lax.rem(q + n_lon - 1, n_lon)),
    )


STRIDE = 45


def peer_count():
    return lax.axis_size("lat") * lax.axis_size("lon")


def own_number():
    return lax.axis_index("lat") * lax.axis_size("lon") + lax.axis_index("lon")


def for_peers(first, last, do):
    n = peer_count()

    def one(k, other):
        do(other)
        other = other + STRIDE
        return jnp.where(other >= n, other - n, other)

    lax.fori_loop(first, last, one, lax.rem(own_number() + STRIDE * first, n))


def greet_all():
    barrier = pltpu.get_barrier_semaphore()

    def signal(other):
        pl.semaphore_signal(
            barrier, inc=1, device_id=other, device_id_type=pl.DeviceIdType.LOGICAL
        )

    for_peers(1, peer_count(), signal)


def greet():
    barrier = pltpu.get_barrier_semaphore()
    for who in neighbours():
        pl.semaphore_signal(barrier, inc=1, device_id=who, device_id_type=MESH)


def greeted(count):
    pl.semaphore_wait(pltpu.get_barrier_semaphore(), count)


def send(src, dst, sems, index, side):
    copy = pltpu.make_async_remote_copy(
        src_ref=src,
        dst_ref=dst,
        send_sem=sems.at[0, index],
        recv_sem=sems.at[1, index],
        device_id=neighbours()[side],
        device_id_type=MESH,
    )
    copy.start()
    return copy


def wait(copies):
    for copy in copies:
        copy.wait()


def lane_iota(shape):
    return lax.broadcasted_iota(jnp.int32, shape, 1)


def turn(x, shift):
    shift %= LANES
    return x if shift == 0 else pltpu.roll(x, shift, 1)


def pack_strip(read, first):
    total = None
    for r in range(ROWS):
        tile = read(r + H)
        at = H * (r + H)
        lanes = lane_iota(tile.shape)
        moved = turn(tile, at - first)
        total = jnp.where((lanes >= at) & (lanes < at + H), moved, 0.0 if total is None else total)
    return total


def halo_tile(west, west_at, east, east_at):
    lanes = lane_iota(west.shape)
    west = turn(west, LANES - H - west_at)
    east = turn(east, -east_at)
    return jnp.where(lanes < H, east, jnp.where(lanes >= LANES - H, west, 0.0))


def corners(west, east):
    lanes = lane_iota(west.shape)
    width = H * H
    top, low = H * ROWS, H * H
    of_west = ((lanes >= top) & (lanes < top + width)) | ((lanes >= low) & (lanes < low + width))
    return jnp.where(of_west, west, turn(east, width))


def own_halo(strips, a, b, rr):
    return halo_tile(strips[2, a:b], H * rr, strips[3, a:b], H * rr)


def corner_halo(strips, a, b, rr):
    slot, at = (5, H * (rr + ROWS)) if rr < H else (6, H * (rr - ROWS))
    slab = strips[slot, a:b]
    return halo_tile(slab, at, slab, at + H * H)


def row_valid(rr):
    n_lat = lax.axis_size("lat")
    row = lax.axis_index("lat") * ROWS + rr - H
    return jnp.where((row >= 0) & (row < ROWS * n_lat), 1.0, 0.0).astype(F32)


def wind_rows(wext, rr, step):
    zonal = wext[rr, 2 * step : 2 * step + 1, :]
    merid = wext[rr, 2 * step + 1 : 2 * step + 2, :]
    return zonal, merid, jnp.abs(zonal), jnp.abs(merid)


def spread(w):
    return jnp.broadcast_to(w, (8, RING))


def forward_row(src, wext, rr, step, emit):
    zonal, merid, az, am = wind_rows(wext, rr, step)
    valid = row_valid(rr)
    wc = spread((1.0 - az - am) * valid)
    wz = spread(az * valid)
    wm = spread(am * valid)
    from_east = spread(zonal) < 0
    from_north = spread(merid) < 0

    def part(c):
        here = src[rr, c : c + 8, :]
        along = jnp.where(from_east, pltpu.roll(here, RING - 1, 1), pltpu.roll(here, 1, 1))
        across = jnp.where(from_north, src[rr + 1, c : c + 8, :], src[rr - 1, c : c + 8, :])
        return wc * here + wz * along + wm * across

    for c in range(0, CH, 16):
        emit(c, part(c), part(c + 8))


def adjoint_row(src, wext, rr, step, emit):
    zonal, _, az, am = wind_rows(wext, rr, step)
    half = 0.5 * row_valid(rr)
    wc = spread((1.0 - az - am) * row_valid(rr))
    we = pltpu.roll(spread(half * (az - zonal)), 1, 1)
    ww = pltpu.roll(spread(half * (az + zonal)), RING - 1, 1)
    _, merid, _, am = wind_rows(wext, rr - 1, step)
    wn = spread(0.5 * row_valid(rr - 1) * (am - merid))
    _, merid, _, am = wind_rows(wext, rr + 1, step)
    ws = spread(0.5 * row_valid(rr + 1) * (am + merid))

    def part(c):
        here = src[rr, c : c + 8, :]
        return (
            wc * here
            + we * pltpu.roll(here, 1, 1)
            + ww * pltpu.roll(here, RING - 1, 1)
            + wn * src[rr - 1, c : c + 8, :]
            + ws * src[rr + 1, c : c + 8, :]
        )

    for c in range(0, CH, 16):
        emit(c, part(c), part(c + 8))


def advance(row, src, dst, wext, step, pairs, base, emit=None):
    def store(rr):
        def put(c, low, high):
            dst[rr, c : c + 8, :] = low
            dst[rr, c + 8 : c + 16, :] = high

        return put

    def body(t, carry):
        for k in range(2):
            rr = base(t) + k
            row(src, wext, rr, step, (emit or store)(rr))
        return carry

    lax.fori_loop(0, pairs, body, 0)


def inner(row, xa, xb, wext, steps, emit):
    src, dst = xa, xb
    for n in range(STEPS):
        first = H + 1 + n
        last = emit if n == STEPS - 1 else None
        advance(row, src, dst, wext, steps[n], 7 - n, lambda t, first=first: first + 2 * t, last)
        src, dst = dst, src


def outer(row, xa, xb, wext, steps, emit):
    src, dst = xa, xb
    for n in range(STEPS):
        low, high = 1 + n, H + ROWS - 1 - n
        last = emit if n == STEPS - 1 else None
        advance(
            row, src, dst, wext, steps[n], 4,
            lambda t, low=low, high=high: 2 * t + jnp.where(t < 2, low, high - 4), last,
        )
        src, dst = dst, src


def cov_pair(base, ext, pat, lhs, cov, adjoint):
    for n in range(2):
        for b in range(2):
            m = (2 * n + b) * CH
            for k in range(OFFS):
                at = base + n + (2 * R - k if adjoint else k)
                at_pat = at if adjoint else base + n
                mask = pat[at_pat, 2 * k + b : 2 * k + b + 1, :]
                mask = jnp.broadcast_to(mask, (16, BLOCK)).astype(BF16)
                rows = ext[at, :, b * BLOCK : (b + 1) * BLOCK].reshape(CH // 16, 16, BLOCK)
                lhs[m : m + CH, k * BLOCK : (k + 1) * BLOCK] = (rows * mask[None]).reshape(CH, BLOCK)
    return jnp.dot(lhs[...], cov[...], preferred_element_type=F32)


def send_pair(ext, sems, index, up, down):
    return (
        send(ext.at[pl.ds(R + up, 2)], ext.at[pl.ds(R + up - ROWS, 2)], sems, index, NORTH),
        send(ext.at[pl.ds(R + down, 2)], ext.at[pl.ds(R + down + ROWS, 2)], sems, index + 1, SOUTH),
    )


def send_rows(field, stage, sems, index, up, down, count, at):
    here = pl.ds(at, count)
    stage[0, at : at + count] = field[H + up : H + up + count, :, 0:COLS].astype(BF16)
    north = send(stage.at[0, here], stage.at[2, here], sems, index, NORTH)
    stage[1, at : at + count] = field[H + down : H + down + count, :, 0:COLS].astype(BF16)
    south = send(stage.at[1, here], stage.at[3, here], sems, index + 1, SOUTH)
    return north, south


def place_rows(field, stage, north_order, south_order):
    low, high = row_valid(0), row_valid(EXT - 1)
    for k in range(H):
        field[k, :, 0:COLS] = stage[2, north_order[k]].astype(F32) * low
        field[ROWS + H + k, :, 0:COLS] = stage[3, south_order[k]].astype(F32) * high


def send_strips(strips, sems, index, put):
    put(0, COLS - LANES, LANES - H)
    east = send(strips.at[0], strips.at[2], sems, index, EAST)
    put(1, 0, 0)
    west = send(strips.at[1], strips.at[3], sems, index + 1, WEST)
    return east, west


def send_corners(strips, sems, index):
    strips[4] = corners(strips[2], strips[3])
    return (
        send(strips.at[4], strips.at[5], sems, index, NORTH),
        send(strips.at[4], strips.at[6], sems, index + 1, SOUTH),
    )


def pattern_table(pattern, table):
    table[...] = jnp.zeros_like(table)
    for k in range(OFFS):
        table[2 * k : 2 * k + 2, 0:ROWS] = pattern[k].astype(F32)
    shape = table.shape
    offset = lax.broadcasted_iota(jnp.int32, shape, 0) // 2 - R
    row = lax.axis_index("lat") * ROWS + lane_iota(shape) + offset
    inside = (row >= 0) & (row < ROWS * lax.axis_size("lat"))
    table[...] = jnp.where(inside, table[...], 0.0)


def records(jac, value, weight, column, count, wide, packed):
    slots = value.shape[0]
    live = lax.broadcasted_iota(jnp.int32, value.shape, 0) < jnp.broadcast_to(count[...], value.shape)
    cell = column[...]
    extra = (
        value[...].astype(F32),
        jnp.where(live, weight[...].astype(F32), 0.0),
        lax.shift_right_logical(cell, 8).astype(F32),
        jnp.bitwise_and(cell, COLS - 1).astype(F32),
    )

    def put(s, low):
        block = jnp.concatenate([jac[s].astype(F32), low], axis=0)
        wide[pl.ds(s, LANES, stride=slots), :] = block.T

    for s in range(4):
        put(s, extra[s])

    def rest(s, carry):
        put(s, jnp.zeros(value.shape, F32))
        return carry

    lax.fori_loop(4, slots, rest, 0)

    def narrow(t, carry):
        at = pl.multiple_of(t * 512, 512)
        packed[pl.ds(at, 512), :] = wide[pl.ds(at, 512), :].astype(BF16)
        return carry

    lax.fori_loop(0, SLOTS // 512, narrow, 0)


def record_copy(packed, rec, sems, other):
    per = SLOTS // peer_count()
    return pltpu.make_async_remote_copy(
        src_ref=packed.at[pl.ds(pl.multiple_of(other * per, per), per)],
        dst_ref=rec.at[pl.ds(pl.multiple_of(own_number() * per, per), per)],
        send_sem=sems.at[0],
        recv_sem=sems.at[1],
        device_id=other,
        device_id_type=pl.DeviceIdType.LOGICAL,
    )


def send_records(packed, rec, sems, first, last):
    for_peers(first, last, lambda other: record_copy(packed, rec, sems, other).start())


def wait_records(packed, rec, sems):
    most = pl.ds(0, SLOTS - SLOTS // peer_count())
    both = pltpu.make_async_remote_copy(
        src_ref=packed.at[most],
        dst_ref=rec.at[most],
        send_sem=sems.at[0],
        recv_sem=sems.at[1],
        device_id=neighbours()[0],
        device_id_type=MESH,
    )
    both.wait_send()
    both.wait_recv()


def forward_kernel(
    ctrl, winds, pattern, cov, jac, value, weight, column, count, fin, wout, pout, rec,
    raw, ext, tables, pf, lhs, covcat, xa, xb, stage, wext, strips, wide_rec, packed, sems, local, rsems,
):
    order = (14, 15, 0, 1, 12, 13, 2, 3, 10, 11, 4, 5, 6, 7, 8, 9)
    greet_all()
    rows_in = {r: pltpu.make_async_copy(ctrl.at[:, r, :], raw.at[r], local.at[0, r]) for r in order}
    winds_in = [
        pltpu.make_async_copy(winds.at[:, r, :], wext.at[H + r, :, pl.ds(0, COLS)], local.at[1, r])
        for r in range(ROWS)
    ]
    for r in order:
        rows_in[r].start()
    for copy in winds_in:
        copy.start()
    pattern_table(pattern, tables.at[0])
    for r in order:
        rows_in[r].wait()
        ext[R + r] = raw[r].astype(BF16)
    for k in range(OFFS):
        covcat[k * BLOCK : (k + 1) * BLOCK, :] = cov[abs(k - R)]
    for r in range(ROWS):
        pf[r] = jnp.broadcast_to(tables[0, :, r : r + 1], (32, BLOCK))
    wait(winds_in)
    greeted(peer_count() - 1)
    chunks = [
        send_pair(ext, sems, 2 * n, up, down)
        for n, (up, down) in enumerate(((14, 0), (12, 2), (10, 4)))
    ]
    wide = pl.ds(0, COLS)
    wind_rows_sent = (
        send(wext.at[pl.ds(ROWS, H), :, wide], wext.at[pl.ds(0, H), :, wide], sems, 6, NORTH),
        send(wext.at[pl.ds(H, H), :, wide], wext.at[pl.ds(ROWS + H, H), :, wide], sems, 7, SOUTH),
    )
    patterns = [
        send(tables.at[0], tables.at[1], sems, 16, NORTH),
        send(tables.at[0], tables.at[2], sems, 17, SOUTH),
    ]
    records(jac, value, weight, column, count, wide_rec, packed)
    per = SLOTS // peer_count()
    mine = pl.ds(pl.multiple_of(own_number() * per, per), per)
    own = pltpu.make_async_copy(packed.at[mine], rec.at[mine], local.at[2, 0])
    own.start()
    send_records(packed, rec, rsems, 1, WAVE)

    def pairs(first, gap):
        def pair(t, carry):
            base = first + gap * t
            y = cov_pair(base, ext, pf, lhs, covcat, False)
            for n in range(2):
                for b in range(2):
                    m = (2 * n + b) * CH
                    xa[H + base + n, :, b * BLOCK : (b + 1) * BLOCK] = y[m : m + CH]
            return carry

        lax.fori_loop(0, 2, pair, 0)

    pairs(6, 2)
    wait(chunks[0])
    pairs(4, 6)
    wait(chunks[1])
    pairs(2, 10)
    near = send_rows(xa, stage, sems, 8, 12, 2, 2, 0)
    wait(chunks[2])
    pairs(0, 14)
    far = send_rows(xa, stage, sems, 10, 14, 0, 2, 2)

    def put(slot, at, first):
        strips[slot, 0:CH] = pack_strip(lambda rr: xa[rr, :, at : at + LANES], first)
        strips[slot, CH : CH + 8] = pack_strip(lambda rr: wext[rr, :, at : at + LANES], first)

    wait(send_strips(strips, sems, 12, put))
    turned = send_corners(strips, sems, 14)
    send_records(packed, rec, rsems, WAVE, peer_count())
    for rr in range(H, H + ROWS):
        xa[rr, :, COLS:RING] = own_halo(strips, 0, CH, rr)
        wext[rr, :, COLS:RING] = own_halo(strips, CH, CH + 8, rr)

    def emit(rr):
        def put(c, low, high):
            raw[rr - H, c : c + 8, :] = low[:, 0:COLS]
            raw[rr - H, c + 8 : c + 16, :] = high[:, 0:COLS]

        return put

    def put_out(first, count, index):
        here = pl.ds(first, count)
        copy = pltpu.make_async_copy(raw.at[here], fin.at[here], local.at[2, index])
        copy.start()
        return copy

    steps = tuple(range(STEPS))
    inner(forward_row, xa, xb, wext, steps, emit)
    outgoing = [put_out(4, 8, 1)]
    wait(near + far + turned + wind_rows_sent)
    place_rows(xa, stage, (0, 1, 2, 3), (2, 3, 0, 1))
    for rr in (*range(H), *range(H + ROWS, EXT)):
        xa[rr, :, COLS:RING] = corner_halo(strips, 0, CH, rr) * row_valid(rr)
        wext[rr, :, COLS:RING] = corner_halo(strips, CH, CH + 8, rr)
    outer(forward_row, xa, xb, wext, steps, emit)
    outgoing += [put_out(0, 4, 2), put_out(12, 4, 3)]
    wout[...] = wext[...]
    wait(patterns)
    pout[...] = tables[...]
    own.wait()
    wait(outgoing)
    wait_records(packed, rec, rsems)


def adjoint_kernel(
    forcing, winds, pattern, cov, ctrl, out,
    ext, pf, lhs, covcat, xa, xb, stage, strips, back, sems, local,
):
    incoming = [
        pltpu.make_async_copy(ctrl.at[:, r, :], back.at[r], local.at[1, r]) for r in range(ROWS)
    ]
    greet()
    fields = [
        pltpu.make_async_copy(
            forcing.at[pl.ds(first, count)],
            xa.at[pl.ds(H + first, count), :, pl.ds(0, COLS)],
            local.at[2, first],
        )
        for first, count in ((12, 4), (0, 4), (4, 8))
    ]
    for copy in fields + incoming:
        copy.start()
    wait(fields)
    strips[0] = pack_strip(lambda rr: xa[rr, :, COLS - LANES : COLS], LANES - H)
    strips[1] = pack_strip(lambda rr: xa[rr, :, 0:LANES], 0)
    greeted(4)
    sides = (
        send(strips.at[0], strips.at[2], sems, 2, EAST),
        send(strips.at[1], strips.at[3], sems, 3, WEST),
    )
    rows = send_rows(xa, stage, sems, 0, 12, 0, 4, 0)
    for k in range(R + 1):
        turned = cov[k].astype(F32).T.astype(BF16)
        for at in {R + k, R - k}:
            covcat[at * BLOCK : (at + 1) * BLOCK, :] = turned
    for i in range(WIDE):
        r = i - R
        slot, lane = (1, r + ROWS) if r < 0 else (2, r - ROWS) if r >= ROWS else (0, r)
        pf[i] = jnp.broadcast_to(pattern[slot, :, lane : lane + 1], (32, BLOCK))
    wait(sides)
    turned = send_corners(strips, sems, 4)
    for rr in range(H, H + ROWS):
        xa[rr, :, COLS:RING] = own_halo(strips, 0, CH, rr)

    def emit(rr):
        def put(c, low, high):
            both = jnp.concatenate([low[:, 0:COLS], high[:, 0:COLS]], axis=0)
            ext[rr - H + R, c : c + 16, :] = both.astype(BF16)

        return put

    steps = tuple(range(STEPS - 1, -1, -1))
    inner(adjoint_row, xa, xb, winds, steps, emit)
    chunks = [send_pair(ext, sems, 6, 10, 4)]
    wait(rows + turned)
    place_rows(xa, stage, (0, 1, 2, 3), (0, 1, 2, 3))
    for rr in (*range(H), *range(H + ROWS, EXT)):
        xa[rr, :, COLS:RING] = corner_halo(strips, 0, CH, rr)
    outer(adjoint_row, xa, xb, winds, steps, emit)
    chunks.append(send_pair(ext, sems, 8, 14, 0))
    chunks.append(send_pair(ext, sems, 10, 12, 2))
    outgoing = []
    wait(incoming)

    def pairs(first, gap):
        def pair(t, carry):
            base = first + gap * t
            y = cov_pair(base, ext, pf, lhs, covcat, True)
            for n in range(2):
                for b in range(2):
                    m = (2 * n + b) * CH
                    lanes = slice(b * BLOCK, (b + 1) * BLOCK)
                    back[base + n, :, lanes] = back[base + n, :, lanes] + y[m : m + CH]
            return carry

        lax.fori_loop(0, 2, pair, 0)
        for r in (first, first + 1, first + gap, first + gap + 1):
            copy = pltpu.make_async_copy(back.at[r], out.at[:, r, :], local.at[0, r])
            copy.start()
            outgoing.append(copy)

    pairs(6, 2)
    wait(chunks[1])
    pairs(4, 6)
    wait(chunks[2])
    pairs(2, 10)
    wait(chunks[0])
    pairs(0, 14)
    wait(outgoing)


def obs_kernel(rec, fin, forcing, forecast, field, f2, r32, aux, ct, rowb, yt, zt, local):
    per = 32
    field_in = pltpu.make_async_copy(fin, field, local.at[ROWS])
    field_in.start()

    def widen(t, carry):
        at = pl.multiple_of(t * 512, 512)
        r32[pl.ds(at, 512), :] = rec[pl.ds(at, 512), :].astype(F32)
        return carry

    lax.fori_loop(0, SLOTS // 512, widen, 0)
    group = lane_iota((per, LANES)) // per
    for k in range(4):
        total = jnp.zeros((per, LANES), F32)
        for q in range(4):
            part = r32[pl.ds(q * per + k, per, stride=4 * per), :]
            total = jnp.where(group == q, turn(part, per * q + per), total)
        aux[k] = total
    field_in.wait()
    outgoing = []
    for r in range(ROWS):
        copy = pltpu.make_async_copy(field.at[r], forecast.at[:, r, :], local.at[r])
        copy.start()
        outgoing.append(copy)
    for r in range(ROWS):
        high = field[r].astype(BF16)
        f2[0, r * CH : (r + 1) * CH, :] = high
        f2[1, r * CH : (r + 1) * CH, :] = (field[r] - high.astype(F32)).astype(BF16)
    sub = lax.broadcasted_iota(jnp.int32, (COLS, TILE), 0).astype(F32)

    def vector(k, t):
        return jnp.concatenate([aux[k, pl.ds(2 * t, 1), :], aux[k, pl.ds(2 * t + 1, 1), :]], axis=1)

    def gather(t, carry):
        at = pl.multiple_of(t * TILE, TILE)
        value, weight, row, col = (vector(k, t) for k in range(4))
        hot = jnp.where(jnp.broadcast_to(col, (COLS, TILE)) == sub, 1.0, 0.0).astype(BF16)
        ct[:, pl.ds(at, TILE)] = hot
        row8 = jnp.broadcast_to(row, (8, TILE))
        rowb[:, pl.ds(at, TILE)] = jnp.broadcast_to(row, (16, TILE)).astype(BF16)
        halves = []
        for part in range(2):
            got = jnp.zeros((CH // 8, 8, TILE), F32)
            for g in range(0, ROWS, GROUP):
                rows = f2[part, g * CH : (g + GROUP) * CH, :]
                some = jnp.dot(rows, hot, preferred_element_type=F32)
                for k in range(GROUP):
                    piece = some[k * CH : (k + 1) * CH].reshape(CH // 8, 8, TILE)
                    got = jnp.where((row8 == float(g + k))[None], piece, got)
            halves.append(got)
        got = (halves[0] + halves[1]).reshape(CH, TILE)
        jac = jnp.concatenate(
            [r32[pl.ds(at, LANES), :].T[0:CH], r32[pl.ds(at + LANES, LANES), :].T[0:CH]], axis=1
        )
        evolved = jnp.sum(jac * got, axis=0, keepdims=True)
        residual = weight * (evolved - value)
        yt[:, pl.ds(at, TILE)] = (jac * residual).astype(BF16)
        return carry

    lax.fori_loop(0, SLOTS // TILE, gather, 0)
    wait(outgoing)

    def scatter(g, carry):
        for k in range(GROUP):
            want = (g * GROUP + k).astype(F32)
            for c in range(0, SLOTS, 512):
                here = jnp.where(rowb[:, c : c + 512].astype(F32) == want, 1.0, 0.0).astype(BF16)
                part = yt[:, c : c + 512].reshape(CH // 16, 16, 512) * here[None]
                zt[k * CH : (k + 1) * CH, c : c + 512] = part.reshape(CH, 512)
        total = lax.dot_general(
            zt[...], ct[...], (((1,), (1,)), ((), ())), preferred_element_type=F32
        )
        for k in range(GROUP):
            field[g * GROUP + k] = total[k * CH : (k + 1) * CH]
        put_out(g).start()
        return carry

    def put_out(g):
        here = pl.ds(g * GROUP, GROUP)
        return pltpu.make_async_copy(field.at[here], forcing.at[here], local.at[g])

    lax.fori_loop(0, ROWS // GROUP, scatter, 0)
    wait([put_out(g) for g in range(ROWS // GROUP)])


def vmem(n):
    return [pl.BlockSpec(memory_space=pltpu.VMEM)] * n


def anywhere(n):
    return [pl.BlockSpec(memory_space=pl.ANY)] * n


def params(**more):
    return pltpu.CompilerParams(vmem_limit_bytes=60 * 1024 * 1024, **more)


def advection_scratch(strip_rows):
    return [
        pltpu.VMEM((EXT, CH, RING), F32),
        pltpu.VMEM((EXT, CH, RING), F32),
        pltpu.VMEM((4, H, CH, COLS), BF16),
        pltpu.VMEM((7, strip_rows, LANES), F32),
    ]


def covariance_scratch(pattern_rows):
    return [
        pltpu.VMEM((pattern_rows, 32, BLOCK), F32),
        pltpu.VMEM((4 * CH, OFFS * BLOCK), BF16),
        pltpu.VMEM((OFFS * BLOCK, BLOCK), BF16),
    ]


def forward_call(*args):
    xa, xb, stage, strips = advection_scratch(CH + 8)
    return pl.pallas_call(
        forward_kernel,
        name="forward",
        out_shape=(
            jax.ShapeDtypeStruct((ROWS, CH, COLS), F32),
            jax.ShapeDtypeStruct((EXT, 8, RING), F32),
            jax.ShapeDtypeStruct((3, 32, LANES), F32),
            jax.ShapeDtypeStruct((SLOTS, LANES), BF16),
        ),
        in_specs=anywhere(2) + vmem(7),
        out_specs=tuple(anywhere(1) + vmem(2) + anywhere(1)),
        scratch_shapes=[
            pltpu.VMEM((ROWS, CH, COLS), F32),
            pltpu.VMEM((WIDE, CH, COLS), BF16),
            pltpu.VMEM((3, 32, LANES), F32),
            *covariance_scratch(ROWS),
            xa,
            xb,
            stage,
            pltpu.VMEM((EXT, 8, RING), F32),
            strips,
            pltpu.VMEM((SLOTS, LANES), F32),
            pltpu.VMEM((SLOTS, LANES), BF16),
            pltpu.SemaphoreType.DMA((2, 18)),
            pltpu.SemaphoreType.DMA((3, ROWS)),
            pltpu.SemaphoreType.DMA((2,)),
        ],
        compiler_params=params(collective_id=0, has_side_effects=True),
        cost_estimate=pl.CostEstimate(
            flops=3_000_000_000, bytes_accessed=16_000_000, transcendentals=0
        ),
    )(*args)


def adjoint_call(forcing, winds, pattern, cov, ctrl):
    xa, xb, stage, strips = advection_scratch(CH)
    return pl.pallas_call(
        adjoint_kernel,
        name="adjoint",
        out_shape=jax.ShapeDtypeStruct((CH, ROWS, COLS), F32),
        in_specs=anywhere(1) + vmem(3) + anywhere(1),
        out_specs=anywhere(1)[0],
        scratch_shapes=[
            pltpu.VMEM((WIDE, CH, COLS), BF16),
            *covariance_scratch(WIDE),
            xa,
            xb,
            stage,
            strips,
            pltpu.VMEM((ROWS, CH, COLS), F32),
            pltpu.SemaphoreType.DMA((2, 12)),
            pltpu.SemaphoreType.DMA((3, ROWS)),
        ],
        compiler_params=params(collective_id=1, has_side_effects=True),
    )(forcing, winds, pattern, cov, ctrl)


def obs_call(rec, fin):
    return pl.pallas_call(
        obs_kernel,
        name="observe",
        out_shape=(
            jax.ShapeDtypeStruct((ROWS, CH, COLS), F32),
            jax.ShapeDtypeStruct((CH, ROWS, COLS), F32),
        ),
        in_specs=vmem(1) + anywhere(1),
        out_specs=tuple(anywhere(2)),
        scratch_shapes=[
            pltpu.VMEM((ROWS, CH, COLS), F32),
            pltpu.VMEM((2, ROWS * CH, COLS), BF16),
            pltpu.VMEM((SLOTS, LANES), F32),
            pltpu.VMEM((4, 32, LANES), F32),
            pltpu.VMEM((COLS, SLOTS), BF16),
            pltpu.VMEM((16, SLOTS), BF16),
            pltpu.VMEM((CH, SLOTS), BF16),
            pltpu.VMEM((GROUP * CH, SLOTS), BF16),
            pltpu.SemaphoreType.DMA((ROWS + 1,)),
        ],
        compiler_params=params(),
    )(rec, fin)


def on_device(
    control, winds, pattern, cov_tables, jacobians, obs_value, obs_weight, obs_column, obs_count
):
    wind2 = winds.reshape(2 * STEPS, ROWS, COLS)
    fin, wext, table, rec = forward_call(
        control,
        wind2,
        jnp.transpose(pattern, (2, 1, 0)),
        cov_tables,
        jnp.transpose(jacobians[0], (1, 2, 0)),
        obs_value[0].T,
        obs_weight[0].T,
        obs_column[0].T,
        obs_count,
    )
    forcing, forecast = obs_call(rec, fin)
    gradient = adjoint_call(forcing, wext, table, cov_tables, control)
    return forecast, gradient


def solution(mesh):
    in_specs = (
        P(None, "lat", "lon"),
        P(None, None, "lat", "lon"),
        P("lat", "lon", None),
        P(),
        P(("lat", "lon"), None, None, None),
        P(("lat", "lon"), None, None),
        P(("lat", "lon"), None, None),
        P(("lat", "lon"), None, None),
        P(("lat", "lon"), None),
    )
    out_specs = (P(None, "lat", "lon"), P(None, "lat", "lon"))
    return jax.shard_map(
        on_device, mesh=mesh, in_specs=in_specs, out_specs=out_specs, check_vma=False
    )
```

```python
import jax
import jax.numpy as jnp
from jax import lax
from jax.experimental import pallas as pl
from jax.experimental.pallas import tpu as pltpu
from jax.sharding import PartitionSpec as P

BLOCK = 128
R = 6
OFFS = 2 * R + 1
STEPS = 4
H = STEPS
ROWS = 16
COLS = 256
CH = 96
EXT = ROWS + 2 * H
WIDE = ROWS + 2 * R
RING = COLS + 128
LANES = 128
SLOTS = 4096
TILE = 256
GROUP = 4
F32 = jnp.float32
BF16 = jnp.bfloat16
MESH = pl.DeviceIdType.MESH
NORTH, SOUTH, EAST, WEST = 0, 1, 2, 3


def neighbours():
    n_lat = lax.axis_size("lat")
    n_lon = lax.axis_size("lon")
    p = lax.axis_index("lat")
    q = lax.axis_index("lon")
    return (
        (lax.rem(p + 1, n_lat), q),
        (lax.rem(p + n_lat - 1, n_lat), q),
        (p, lax.rem(q + 1, n_lon)),
        (p, lax.rem(q + n_lon - 1, n_lon)),
    )


STRIDE = 45


def peer_count():
    return lax.axis_size("lat") * lax.axis_size("lon")


def own_number():
    return lax.axis_index("lat") * lax.axis_size("lon") + lax.axis_index("lon")


def for_peers(first, last, do):
    n = peer_count()

    def one(k, other):
        do(other)
        other = other + STRIDE
        return jnp.where(other >= n, other - n, other)

    lax.fori_loop(first, last, one, lax.rem(own_number() + STRIDE * first, n))


def greet_all():
    barrier = pltpu.get_barrier_semaphore()

    def signal(other):
        pl.semaphore_signal(
            barrier, inc=1, device_id=other, device_id_type=pl.DeviceIdType.LOGICAL
        )

    for_peers(1, peer_count(), signal)


def greet():
    barrier = pltpu.get_barrier_semaphore()
    for who in neighbours():
        pl.semaphore_signal(barrier, inc=1, device_id=who, device_id_type=MESH)


def greeted(count):
    pl.semaphore_wait(pltpu.get_barrier_semaphore(), count)


def send(src, dst, sems, index, side):
    copy = pltpu.make_async_remote_copy(
        src_ref=src,
        dst_ref=dst,
        send_sem=sems.at[0, index],
        recv_sem=sems.at[1, index],
        device_id=neighbours()[side],
        device_id_type=MESH,
    )
    copy.start()
    return copy


def wait(copies):
    for copy in copies:
        copy.wait()


def lane_iota(shape):
    return lax.broadcasted_iota(jnp.int32, shape, 1)


def turn(x, shift):
    shift %= LANES
    return x if shift == 0 else pltpu.roll(x, shift, 1)


def pack_strip(read, first):
    total = None
    for r in range(ROWS):
        tile = read(r + H)
        at = H * (r + H)
        lanes = lane_iota(tile.shape)
        moved = turn(tile, at - first)
        total = jnp.where((lanes >= at) & (lanes < at + H), moved, 0.0 if total is None else total)
    return total


def halo_tile(west, west_at, east, east_at):
    lanes = lane_iota(west.shape)
    west = turn(west, LANES - H - west_at)
    east = turn(east, -east_at)
    return jnp.where(lanes < H, east, jnp.where(lanes >= LANES - H, west, 0.0))


def corners(west, east):
    lanes = lane_iota(west.shape)
    width = H * H
    top, low = H * ROWS, H * H
    of_west = ((lanes >= top) & (lanes < top + width)) | ((lanes >= low) & (lanes < low + width))
    return jnp.where(of_west, west, turn(east, width))


def own_halo(strips, a, b, rr):
    return halo_tile(strips[2, a:b], H * rr, strips[3, a:b], H * rr)


def corner_halo(strips, a, b, rr):
    slot, at = (5, H * (rr + ROWS)) if rr < H else (6, H * (rr - ROWS))
    slab = strips[slot, a:b]
    return halo_tile(slab, at, slab, at + H * H)


def row_valid(rr):
    n_lat = lax.axis_size("lat")
    row = lax.axis_index("lat") * ROWS + rr - H
    return jnp.where((row >= 0) & (row < ROWS * n_lat), 1.0, 0.0).astype(F32)


def wind_rows(wext, rr, step):
    zonal = wext[rr, 2 * step : 2 * step + 1, :]
    merid = wext[rr, 2 * step + 1 : 2 * step + 2, :]
    return zonal, merid, jnp.abs(zonal), jnp.abs(merid)


def spread(w):
    return jnp.broadcast_to(w, (8, RING))


def forward_row(src, wext, rr, step, emit):
    zonal, merid, az, am = wind_rows(wext, rr, step)
    valid = row_valid(rr)
    wc = spread((1.0 - az - am) * valid)
    wz = spread(az * valid)
    wm = spread(am * valid)
    from_east = spread(zonal) < 0
    from_north = spread(merid) < 0

    def part(c):
        here = src[rr, c : c + 8, :]
        along = jnp.where(from_east, pltpu.roll(here, RING - 1, 1), pltpu.roll(here, 1, 1))
        across = jnp.where(from_north, src[rr + 1, c : c + 8, :], src[rr - 1, c : c + 8, :])
        return wc * here + wz * along + wm * across

    for c in range(0, CH, 16):
        emit(c, part(c), part(c + 8))


def adjoint_row(src, wext, rr, step, emit):
    zonal, _, az, am = wind_rows(wext, rr, step)
    half = 0.5 * row_valid(rr)
    wc = spread((1.0 - az - am) * row_valid(rr))
    we = pltpu.roll(spread(half * (az - zonal)), 1, 1)
    ww = pltpu.roll(spread(half * (az + zonal)), RING - 1, 1)
    _, merid, _, am = wind_rows(wext, rr - 1, step)
    wn = spread(0.5 * row_valid(rr - 1) * (am - merid))
    _, merid, _, am = wind_rows(wext, rr + 1, step)
    ws = spread(0.5 * row_valid(rr + 1) * (am + merid))

    def part(c):
        here = src[rr, c : c + 8, :]
        return (
            wc * here
            + we * pltpu.roll(here, 1, 1)
            + ww * pltpu.roll(here, RING - 1, 1)
            + wn * src[rr - 1, c : c + 8, :]
            + ws * src[rr + 1, c : c + 8, :]
        )

    for c in range(0, CH, 16):
        emit(c, part(c), part(c + 8))


def advance(row, src, dst, wext, step, turns, per, base, emit=None):
    def store(rr):
        def put(c, low, high):
            dst[rr, c : c + 8, :] = low
            dst[rr, c + 8 : c + 16, :] = high

        return put

    def body(t, carry):
        for k in range(per):
            rr = base(t) + k
            row(src, wext, rr, step, (emit or store)(rr))
        return carry

    lax.fori_loop(0, turns, body, 0)


def inner(row, xa, xb, wext, steps, emit):
    src, dst = xa, xb
    for n in range(STEPS):
        first = H + 1 + n
        last = emit if n == STEPS - 1 else None
        count = ROWS - 2 - 2 * n
        per = 4 if count % 4 == 0 else 2
        advance(
            row, src, dst, wext, steps[n], count // per, per,
            lambda t, first=first, per=per: first + per * t, last,
        )
        src, dst = dst, src


def outer(row, xa, xb, wext, steps, emit):
    src, dst = xa, xb
    for n in range(STEPS):
        low, high = 1 + n, H + ROWS - 1 - n
        last = emit if n == STEPS - 1 else None
        advance(
            row, src, dst, wext, steps[n], 2, 4,
            lambda t, low=low, high=high: low + t * (high - low), last,
        )
        src, dst = dst, src


def cov_pair(base, ext, pat, lhs, cov, adjoint):
    for n in range(2):
        for b in range(2):
            m = (2 * n + b) * CH
            for k in range(OFFS):
                at = base + n + (2 * R - k if adjoint else k)
                at_pat = at if adjoint else base + n
                mask = pat[at_pat, 2 * k + b : 2 * k + b + 1, :]
                mask = jnp.broadcast_to(mask, (16, BLOCK)).astype(BF16)
                rows = ext[at, :, b * BLOCK : (b + 1) * BLOCK].reshape(CH // 16, 16, BLOCK)
                lhs[m : m + CH, k * BLOCK : (k + 1) * BLOCK] = (rows * mask[None]).reshape(CH, BLOCK)
    return jnp.dot(lhs[...], cov[...], preferred_element_type=F32)


def send_pair(ext, sems, index, up, down):
    return (
        send(ext.at[pl.ds(R + up, 2)], ext.at[pl.ds(R + up - ROWS, 2)], sems, index, NORTH),
        send(ext.at[pl.ds(R + down, 2)], ext.at[pl.ds(R + down + ROWS, 2)], sems, index + 1, SOUTH),
    )


def send_rows(field, stage, sems, index, up, down, count, at):
    here = pl.ds(at, count)
    stage[0, at : at + count] = field[H + up : H + up + count, :, 0:COLS].astype(BF16)
    north = send(stage.at[0, here], stage.at[2, here], sems, index, NORTH)
    stage[1, at : at + count] = field[H + down : H + down + count, :, 0:COLS].astype(BF16)
    south = send(stage.at[1, here], stage.at[3, here], sems, index + 1, SOUTH)
    return north, south


def place_rows(field, stage, north_order, south_order):
    low, high = row_valid(0), row_valid(EXT - 1)
    for k in range(H):
        field[k, :, 0:COLS] = stage[2, north_order[k]].astype(F32) * low
        field[ROWS + H + k, :, 0:COLS] = stage[3, south_order[k]].astype(F32) * high


def send_strips(strips, sems, index, put):
    put(0, COLS - LANES, LANES - H)
    east = send(strips.at[0], strips.at[2], sems, index, EAST)
    put(1, 0, 0)
    west = send(strips.at[1], strips.at[3], sems, index + 1, WEST)
    return east, west


def send_corners(strips, sems, index):
    strips[4] = corners(strips[2], strips[3])
    return (
        send(strips.at[4], strips.at[5], sems, index, NORTH),
        send(strips.at[4], strips.at[6], sems, index + 1, SOUTH),
    )


def pattern_table(pattern, table):
    table[...] = jnp.zeros_like(table)
    for k in range(OFFS):
        table[2 * k : 2 * k + 2, 0:ROWS] = pattern[k].astype(F32)
    shape = table.shape
    offset = lax.broadcasted_iota(jnp.int32, shape, 0) // 2 - R
    row = lax.axis_index("lat") * ROWS + lane_iota(shape) + offset
    inside = (row >= 0) & (row < ROWS * lax.axis_size("lat"))
    table[...] = jnp.where(inside, table[...], 0.0)


def records(jac, value, weight, column, count, wide, packed):
    slots = value.shape[0]
    live = lax.broadcasted_iota(jnp.int32, value.shape, 0) < jnp.broadcast_to(count[...], value.shape)
    cell = column[...]
    extra = (
        value[...].astype(F32),
        jnp.where(live, weight[...].astype(F32), 0.0),
        lax.shift_right_logical(cell, 8).astype(F32),
        jnp.bitwise_and(cell, COLS - 1).astype(F32),
    )

    def put(s, low):
        block = jnp.concatenate([jac[s].astype(F32), low], axis=0)
        wide[pl.ds(s, LANES, stride=slots), :] = block.T

    for s in range(4):
        put(s, extra[s])

    def rest(s, carry):
        put(s, jnp.zeros(value.shape, F32))
        return carry

    lax.fori_loop(4, slots, rest, 0)

    def narrow(t, carry):
        at = pl.multiple_of(t * 512, 512)
        packed[pl.ds(at, 512), :] = wide[pl.ds(at, 512), :].astype(BF16)
        return carry

    lax.fori_loop(0, SLOTS // 512, narrow, 0)


def record_copy(packed, rec, sems, other):
    per = SLOTS // peer_count()
    return pltpu.make_async_remote_copy(
        src_ref=packed.at[pl.ds(pl.multiple_of(other * per, per), per)],
        dst_ref=rec.at[pl.ds(pl.multiple_of(own_number() * per, per), per)],
        send_sem=sems.at[0],
        recv_sem=sems.at[1],
        device_id=other,
        device_id_type=pl.DeviceIdType.LOGICAL,
    )


def send_records(packed, rec, sems, first, last):
    for_peers(first, last, lambda other: record_copy(packed, rec, sems, other).start())


def wait_records(packed, rec, sems):
    most = pl.ds(0, SLOTS - SLOTS // peer_count())
    both = pltpu.make_async_remote_copy(
        src_ref=packed.at[most],
        dst_ref=rec.at[most],
        send_sem=sems.at[0],
        recv_sem=sems.at[1],
        device_id=neighbours()[0],
        device_id_type=MESH,
    )
    both.wait_send()
    both.wait_recv()


def forward_kernel(
    ctrl, winds, pattern, cov, jac, value, weight, column, count, fin, wout, pout, rec,
    raw, ext, tables, pf, lhs, covcat, xa, xb, stage, wext, strips, wide_rec, packed, sems, local, rsems,
):
    order = (14, 15, 0, 1, 12, 13, 2, 3, 10, 11, 4, 5, 6, 7, 8, 9)
    rows_in = {r: pltpu.make_async_copy(ctrl.at[:, r, :], raw.at[r], local.at[0, r]) for r in order}
    winds_in = [
        pltpu.make_async_copy(winds.at[:, r, :], wext.at[H + r, :, pl.ds(0, COLS)], local.at[1, r])
        for r in range(ROWS)
    ]
    for r in order:
        rows_in[r].start()
    for copy in winds_in:
        copy.start()
    greet_all()
    pattern_table(pattern, tables.at[0])
    for r in order:
        rows_in[r].wait()
        ext[R + r] = raw[r].astype(BF16)
    for k in range(OFFS):
        covcat[k * BLOCK : (k + 1) * BLOCK, :] = cov[abs(k - R)]
    for r in range(ROWS):
        pf[r] = jnp.broadcast_to(tables[0, :, r : r + 1], (32, BLOCK))
    wait(winds_in)
    greeted(peer_count() - 1)
    chunks = [
        send_pair(ext, sems, 2 * n, up, down)
        for n, (up, down) in enumerate(((14, 0), (12, 2), (10, 4)))
    ]
    wide = pl.ds(0, COLS)
    wind_rows_sent = (
        send(wext.at[pl.ds(ROWS, H), :, wide], wext.at[pl.ds(0, H), :, wide], sems, 6, NORTH),
        send(wext.at[pl.ds(H, H), :, wide], wext.at[pl.ds(ROWS + H, H), :, wide], sems, 7, SOUTH),
    )
    patterns = [
        send(tables.at[0], tables.at[1], sems, 16, NORTH),
        send(tables.at[0], tables.at[2], sems, 17, SOUTH),
    ]
    records(jac, value, weight, column, count, wide_rec, packed)
    per = SLOTS // peer_count()
    mine = pl.ds(pl.multiple_of(own_number() * per, per), per)
    own = pltpu.make_async_copy(packed.at[mine], rec.at[mine], local.at[2, 0])
    own.start()

    def pairs(first, gap):
        for t in range(2):
            base = first + gap * t
            y = cov_pair(base, ext, pf, lhs.at[t], covcat, False)
            for n in range(2):
                for b in range(2):
                    m = (2 * n + b) * CH
                    xa[H + base + n, :, b * BLOCK : (b + 1) * BLOCK] = y[m : m + CH]

    pairs(6, 2)
    wait(chunks[0])
    pairs(4, 6)
    wait(chunks[1])
    pairs(2, 10)
    near = send_rows(xa, stage, sems, 8, 12, 2, 2, 0)
    wait(chunks[2])
    pairs(0, 14)
    far = send_rows(xa, stage, sems, 10, 14, 0, 2, 2)

    def put(slot, at, first):
        strips[slot, 0:CH] = pack_strip(lambda rr: xa[rr, :, at : at + LANES], first)
        strips[slot, CH : CH + 8] = pack_strip(lambda rr: wext[rr, :, at : at + LANES], first)

    wait(send_strips(strips, sems, 12, put))
    turned = send_corners(strips, sems, 14)
    send_records(packed, rec, rsems, 1, peer_count())
    for rr in range(H, H + ROWS):
        xa[rr, :, COLS:RING] = own_halo(strips, 0, CH, rr)
        wext[rr, :, COLS:RING] = own_halo(strips, CH, CH + 8, rr)

    def emit(rr):
        def put(c, low, high):
            raw[rr - H, c : c + 8, :] = low[:, 0:COLS]
            raw[rr - H, c + 8 : c + 16, :] = high[:, 0:COLS]

        return put

    def put_out(first, count, index):
        here = pl.ds(first, count)
        copy = pltpu.make_async_copy(raw.at[here], fin.at[here], local.at[2, index])
        copy.start()
        return copy

    steps = tuple(range(STEPS))
    inner(forward_row, xa, xb, wext, steps, emit)
    outgoing = [put_out(4, 8, 1)]
    wait(near + far + turned + wind_rows_sent)
    place_rows(xa, stage, (0, 1, 2, 3), (2, 3, 0, 1))
    for rr in (*range(H), *range(H + ROWS, EXT)):
        xa[rr, :, COLS:RING] = corner_halo(strips, 0, CH, rr) * row_valid(rr)
        wext[rr, :, COLS:RING] = corner_halo(strips, CH, CH + 8, rr)
    outer(forward_row, xa, xb, wext, steps, emit)
    outgoing += [put_out(0, 4, 2), put_out(12, 4, 3)]
    wout[...] = wext[...]
    wait(patterns)
    pout[...] = tables[...]
    own.wait()
    wait(outgoing)
    wait_records(packed, rec, rsems)


def adjoint_kernel(
    forcing, winds, pattern, cov, ctrl, out,
    ext, pf, lhs, covcat, xa, xb, stage, strips, back, sems, local,
):
    incoming = [
        pltpu.make_async_copy(ctrl.at[:, r, :], back.at[r], local.at[1, r]) for r in range(ROWS)
    ]
    greet()
    fields = [
        pltpu.make_async_copy(
            forcing.at[pl.ds(first, count)],
            xa.at[pl.ds(H + first, count), :, pl.ds(0, COLS)],
            local.at[2, first],
        )
        for first, count in ((12, 4), (0, 4), (4, 8))
    ]
    for copy in fields + incoming:
        copy.start()
    wait(fields)
    strips[0] = pack_strip(lambda rr: xa[rr, :, COLS - LANES : COLS], LANES - H)
    strips[1] = pack_strip(lambda rr: xa[rr, :, 0:LANES], 0)
    greeted(4)
    sides = (
        send(strips.at[0], strips.at[2], sems, 2, EAST),
        send(strips.at[1], strips.at[3], sems, 3, WEST),
    )
    rows = send_rows(xa, stage, sems, 0, 12, 0, 4, 0)
    for k in range(R + 1):
        turned = cov[k].astype(F32).T.astype(BF16)
        for at in {R + k, R - k}:
            covcat[at * BLOCK : (at + 1) * BLOCK, :] = turned
    for i in range(WIDE):
        r = i - R
        slot, lane = (1, r + ROWS) if r < 0 else (2, r - ROWS) if r >= ROWS else (0, r)
        pf[i] = jnp.broadcast_to(pattern[slot, :, lane : lane + 1], (32, BLOCK))
    wait(sides)
    turned = send_corners(strips, sems, 4)
    for rr in range(H, H + ROWS):
        xa[rr, :, COLS:RING] = own_halo(strips, 0, CH, rr)

    def emit(rr):
        def put(c, low, high):
            both = jnp.concatenate([low[:, 0:COLS], high[:, 0:COLS]], axis=0)
            ext[rr - H + R, c : c + 16, :] = both.astype(BF16)

        return put

    steps = tuple(range(STEPS - 1, -1, -1))
    inner(adjoint_row, xa, xb, winds, steps, emit)
    chunks = [send_pair(ext, sems, 6, 10, 4)]
    wait(rows + turned)
    place_rows(xa, stage, (0, 1, 2, 3), (0, 1, 2, 3))
    for rr in (*range(H), *range(H + ROWS, EXT)):
        xa[rr, :, COLS:RING] = corner_halo(strips, 0, CH, rr)
    outer(adjoint_row, xa, xb, winds, steps, emit)
    chunks.append(send_pair(ext, sems, 8, 14, 0))
    chunks.append(send_pair(ext, sems, 10, 12, 2))
    outgoing = []
    wait(incoming)

    def pairs(first, gap):
        for t in range(2):
            base = first + gap * t
            y = cov_pair(base, ext, pf, lhs.at[t], covcat, True)
            for n in range(2):
                for b in range(2):
                    m = (2 * n + b) * CH
                    lanes = slice(b * BLOCK, (b + 1) * BLOCK)
                    back[base + n, :, lanes] = back[base + n, :, lanes] + y[m : m + CH]
        for r in (first, first + 1, first + gap, first + gap + 1):
            copy = pltpu.make_async_copy(back.at[r], out.at[:, r, :], local.at[0, r])
            copy.start()
            outgoing.append(copy)

    pairs(6, 2)
    wait(chunks[1])
    pairs(4, 6)
    wait(chunks[2])
    pairs(2, 10)
    wait(chunks[0])
    pairs(0, 14)
    wait(outgoing)


def obs_kernel(rec, fin, forcing, forecast, field, f2, r32, aux, ct, rowb, yt, zt, local):
    per = 32
    field_in = pltpu.make_async_copy(fin, field, local.at[ROWS])
    field_in.start()

    def widen(t, carry):
        at = pl.multiple_of(t * 512, 512)
        r32[pl.ds(at, 512), :] = rec[pl.ds(at, 512), :].astype(F32)
        return carry

    lax.fori_loop(0, SLOTS // 512, widen, 0)
    group = lane_iota((per, LANES)) // per
    for k in range(4):
        total = jnp.zeros((per, LANES), F32)
        for q in range(4):
            part = r32[pl.ds(q * per + k, per, stride=4 * per), :]
            total = jnp.where(group == q, turn(part, per * q + per), total)
        aux[k] = total
    field_in.wait()
    outgoing = []
    for r in range(ROWS):
        copy = pltpu.make_async_copy(field.at[r], forecast.at[:, r, :], local.at[r])
        copy.start()
        outgoing.append(copy)
    for r in range(ROWS):
        high = field[r].astype(BF16)
        f2[0, r * CH : (r + 1) * CH, :] = high
        f2[1, r * CH : (r + 1) * CH, :] = (field[r] - high.astype(F32)).astype(BF16)
    sub = lax.broadcasted_iota(jnp.int32, (COLS, TILE), 0).astype(F32)

    def vector(k, t):
        return jnp.concatenate([aux[k, pl.ds(2 * t, 1), :], aux[k, pl.ds(2 * t + 1, 1), :]], axis=1)

    def gather(t):
        at = pl.multiple_of(t * TILE, TILE)
        value, weight, row, col = (vector(k, t) for k in range(4))
        hot = jnp.where(jnp.broadcast_to(col, (COLS, TILE)) == sub, 1.0, 0.0).astype(BF16)
        ct[:, pl.ds(at, TILE)] = hot
        row8 = jnp.broadcast_to(row, (8, TILE))
        rowb[:, pl.ds(at, TILE)] = jnp.broadcast_to(row, (16, TILE)).astype(BF16)
        halves = []
        for part in range(2):
            got = jnp.zeros((CH // 8, 8, TILE), F32)
            for g in range(0, ROWS, GROUP):
                rows = f2[part, g * CH : (g + GROUP) * CH, :]
                some = jnp.dot(rows, hot, preferred_element_type=F32)
                for k in range(GROUP):
                    piece = some[k * CH : (k + 1) * CH].reshape(CH // 8, 8, TILE)
                    got = jnp.where((row8 == float(g + k))[None], piece, got)
            halves.append(got)
        got = (halves[0] + halves[1]).reshape(CH, TILE)
        jac = jnp.concatenate(
            [r32[pl.ds(at, LANES), :].T[0:CH], r32[pl.ds(at + LANES, LANES), :].T[0:CH]], axis=1
        )
        evolved = jnp.sum(jac * got, axis=0, keepdims=True)
        residual = weight * (evolved - value)
        yt[:, pl.ds(at, TILE)] = (jac * residual).astype(BF16)

    def two_tiles(t, carry):
        gather(2 * t)
        gather(2 * t + 1)
        return carry

    lax.fori_loop(0, SLOTS // TILE // 2, two_tiles, 0)
    wait(outgoing)

    def scatter(g, zt):
        for k in range(GROUP):
            want = float(g * GROUP + k)
            for c in range(0, SLOTS, 512):
                here = jnp.where(rowb[:, c : c + 512].astype(F32) == want, 1.0, 0.0).astype(BF16)
                part = yt[:, c : c + 512].reshape(CH // 16, 16, 512) * here[None]
                zt[k * CH : (k + 1) * CH, c : c + 512] = part.reshape(CH, 512)
        total = lax.dot_general(
            zt[...], ct[...], (((1,), (1,)), ((), ())), preferred_element_type=F32
        )
        for k in range(GROUP):
            field[g * GROUP + k] = total[k * CH : (k + 1) * CH]
        put_out(g).start()

    def put_out(g):
        here = pl.ds(g * GROUP, GROUP)
        return pltpu.make_async_copy(field.at[here], forcing.at[here], local.at[g])

    for g in range(ROWS // GROUP):
        scatter(g, zt.at[g % 2])
    wait([put_out(g) for g in range(ROWS // GROUP)])


def vmem(n):
    return [pl.BlockSpec(memory_space=pltpu.VMEM)] * n


def anywhere(n):
    return [pl.BlockSpec(memory_space=pl.ANY)] * n


def params(**more):
    return pltpu.CompilerParams(vmem_limit_bytes=60 * 1024 * 1024, **more)


def advection_scratch(strip_rows):
    return [
        pltpu.VMEM((EXT, CH, RING), F32),
        pltpu.VMEM((EXT, CH, RING), F32),
        pltpu.VMEM((4, H, CH, COLS), BF16),
        pltpu.VMEM((7, strip_rows, LANES), F32),
    ]


def covariance_scratch(pattern_rows):
    return [
        pltpu.VMEM((pattern_rows, 32, BLOCK), F32),
        pltpu.VMEM((2, 4 * CH, OFFS * BLOCK), BF16),
        pltpu.VMEM((OFFS * BLOCK, BLOCK), BF16),
    ]


def forward_call(*args):
    xa, xb, stage, strips = advection_scratch(CH + 8)
    return pl.pallas_call(
        forward_kernel,
        name="forward",
        out_shape=(
            jax.ShapeDtypeStruct((ROWS, CH, COLS), F32),
            jax.ShapeDtypeStruct((EXT, 8, RING), F32),
            jax.ShapeDtypeStruct((3, 32, LANES), F32),
            jax.ShapeDtypeStruct((SLOTS, LANES), BF16),
        ),
        in_specs=anywhere(2) + vmem(7),
        out_specs=tuple(anywhere(1) + vmem(2) + anywhere(1)),
        scratch_shapes=[
            pltpu.VMEM((ROWS, CH, COLS), F32),
            pltpu.VMEM((WIDE, CH, COLS), BF16),
            pltpu.VMEM((3, 32, LANES), F32),
            *covariance_scratch(ROWS),
            xa,
            xb,
            stage,
            pltpu.VMEM((EXT, 8, RING), F32),
            strips,
            pltpu.VMEM((SLOTS, LANES), F32),
            pltpu.VMEM((SLOTS, LANES), BF16),
            pltpu.SemaphoreType.DMA((2, 18)),
            pltpu.SemaphoreType.DMA((3, ROWS)),
            pltpu.SemaphoreType.DMA((2,)),
        ],
        compiler_params=params(collective_id=0, has_side_effects=True),
        cost_estimate=pl.CostEstimate(
            flops=3_000_000_000, bytes_accessed=16_000_000, transcendentals=0
        ),
    )(*args)


def adjoint_call(forcing, winds, pattern, cov, ctrl):
    xa, xb, stage, strips = advection_scratch(CH)
    return pl.pallas_call(
        adjoint_kernel,
        name="adjoint",
        out_shape=jax.ShapeDtypeStruct((CH, ROWS, COLS), F32),
        in_specs=anywhere(1) + vmem(3) + anywhere(1),
        out_specs=anywhere(1)[0],
        scratch_shapes=[
            pltpu.VMEM((WIDE, CH, COLS), BF16),
            *covariance_scratch(WIDE),
            xa,
            xb,
            stage,
            strips,
            pltpu.VMEM((ROWS, CH, COLS), F32),
            pltpu.SemaphoreType.DMA((2, 12)),
            pltpu.SemaphoreType.DMA((3, ROWS)),
        ],
        compiler_params=params(collective_id=1, has_side_effects=True),
    )(forcing, winds, pattern, cov, ctrl)


PIECES = 8


def copy_kernel(field, out, held, sems):
    share = CH // PIECES
    pieces = [pl.ds(n * share, share) for n in range(PIECES)]
    inward = [own_copy(field.at[p], held.at[p], sems.at[0, n]) for n, p in enumerate(pieces)]
    outward = []
    for n, p in enumerate(pieces):
        inward[n].wait()
        outward.append(own_copy(held.at[p], out.at[p], sems.at[1, n]))
    wait(outward)


def own_copy(src, dst, sem):
    copy = pltpu.make_async_copy(src, dst, sem)
    copy.start()
    return copy


def copy_call(field):
    return pl.pallas_call(
        copy_kernel,
        name="copy_out",
        out_shape=jax.ShapeDtypeStruct((CH, ROWS, COLS), F32),
        in_specs=anywhere(1),
        out_specs=anywhere(1)[0],
        scratch_shapes=[pltpu.VMEM((CH, ROWS, COLS), F32), pltpu.SemaphoreType.DMA((2, PIECES))],
        compiler_params=params(),
    )(field)


def obs_call(rec, fin):
    return pl.pallas_call(
        obs_kernel,
        name="observe",
        out_shape=(
            jax.ShapeDtypeStruct((ROWS, CH, COLS), F32),
            jax.ShapeDtypeStruct((CH, ROWS, COLS), F32),
        ),
        in_specs=vmem(1) + anywhere(1),
        out_specs=tuple(anywhere(2)),
        scratch_shapes=[
            pltpu.VMEM((ROWS, CH, COLS), F32),
            pltpu.VMEM((2, ROWS * CH, COLS), BF16),
            pltpu.VMEM((SLOTS, LANES), F32),
            pltpu.VMEM((4, 32, LANES), F32),
            pltpu.VMEM((COLS, SLOTS), BF16),
            pltpu.VMEM((16, SLOTS), BF16),
            pltpu.VMEM((CH, SLOTS), BF16),
            pltpu.VMEM((2, GROUP * CH, SLOTS), BF16),
            pltpu.SemaphoreType.DMA((ROWS + 1,)),
        ],
        compiler_params=params(),
    )(rec, fin)


def on_device(
    control, winds, pattern, cov_tables, jacobians, obs_value, obs_weight, obs_column, obs_count
):
    wind2 = winds.reshape(2 * STEPS, ROWS, COLS)
    fin, wext, table, rec = forward_call(
        control,
        wind2,
        jnp.transpose(pattern, (2, 1, 0)),
        cov_tables,
        jnp.transpose(jacobians[0], (1, 2, 0)),
        obs_value[0].T,
        obs_weight[0].T,
        obs_column[0].T,
        obs_count,
    )
    forcing, forecast = obs_call(rec, fin)
    gradient = adjoint_call(forcing, wext, table, cov_tables, control)
    return forecast, copy_call(gradient)


def solution(mesh):
    in_specs = (
        P(None, "lat", "lon"),
        P(None, None, "lat", "lon"),
        P("lat", "lon", None),
        P(),
        P(("lat", "lon"), None, None, None),
        P(("lat", "lon"), None, None),
        P(("lat", "lon"), None, None),
        P(("lat", "lon"), None, None),
        P(("lat", "lon"), None),
    )
    out_specs = (P(None, "lat", "lon"), P(None, "lat", "lon"))
    return jax.shard_map(
        on_device, mesh=mesh, in_specs=in_specs, out_specs=out_specs, check_vma=False
    )
```

```python
import jax
import jax.numpy as jnp
from jax import lax
from jax.experimental import pallas as pl
from jax.experimental.pallas import tpu as pltpu
from jax.sharding import PartitionSpec as P

BLOCK = 128
R = 6
OFFS = 2 * R + 1
STEPS = 4
H = STEPS
ROWS = 16
COLS = 256
CH = 96
EXT = ROWS + 2 * H
WIDE = ROWS + 2 * R
RING = COLS + 128
LANES = 128
SLOTS = 4096
TILE = 256
GROUP = 4
F32 = jnp.float32
BF16 = jnp.bfloat16
MESH = pl.DeviceIdType.MESH
NORTH, SOUTH, EAST, WEST = 0, 1, 2, 3


def neighbours():
    n_lat = lax.axis_size("lat")
    n_lon = lax.axis_size("lon")
    p = lax.axis_index("lat")
    q = lax.axis_index("lon")
    return (
        (lax.rem(p + 1, n_lat), q),
        (lax.rem(p + n_lat - 1, n_lat), q),
        (p, lax.rem(q + 1, n_lon)),
        (p, lax.rem(q + n_lon - 1, n_lon)),
    )


STRIDE = 45


def peer_count():
    return lax.axis_size("lat") * lax.axis_size("lon")


def own_number():
    return lax.axis_index("lat") * lax.axis_size("lon") + lax.axis_index("lon")


def for_peers(first, last, do):
    n = peer_count()

    def one(k, other):
        do(other)
        other = other + STRIDE
        return jnp.where(other >= n, other - n, other)

    lax.fori_loop(first, last, one, lax.rem(own_number() + STRIDE * first, n))


def greet_all():
    barrier = pltpu.get_barrier_semaphore()

    def signal(other):
        pl.semaphore_signal(
            barrier, inc=1, device_id=other, device_id_type=pl.DeviceIdType.LOGICAL
        )

    for_peers(1, peer_count(), signal)


def greet():
    barrier = pltpu.get_barrier_semaphore()
    for who in neighbours():
        pl.semaphore_signal(barrier, inc=1, device_id=who, device_id_type=MESH)


def greeted(count):
    pl.semaphore_wait(pltpu.get_barrier_semaphore(), count)


def send(src, dst, sems, index, side):
    copy = pltpu.make_async_remote_copy(
        src_ref=src,
        dst_ref=dst,
        send_sem=sems.at[0, index],
        recv_sem=sems.at[1, index],
        device_id=neighbours()[side],
        device_id_type=MESH,
    )
    copy.start()
    return copy


def wait(copies):
    for copy in copies:
        copy.wait()


def lane_iota(shape):
    return lax.broadcasted_iota(jnp.int32, shape, 1)


def turn(x, shift):
    shift %= LANES
    return x if shift == 0 else pltpu.roll(x, shift, 1)


def pack_strip(read, first):
    total = None
    for r in range(ROWS):
        tile = read(r + H)
        at = H * (r + H)
        lanes = lane_iota(tile.shape)
        moved = turn(tile, at - first)
        total = jnp.where((lanes >= at) & (lanes < at + H), moved, 0.0 if total is None else total)
    return total


def halo_tile(west, west_at, east, east_at):
    lanes = lane_iota(west.shape)
    west = turn(west, LANES - H - west_at)
    east = turn(east, -east_at)
    return jnp.where(lanes < H, east, jnp.where(lanes >= LANES - H, west, 0.0))


def corners(west, east):
    lanes = lane_iota(west.shape)
    width = H * H
    top, low = H * ROWS, H * H
    of_west = ((lanes >= top) & (lanes < top + width)) | ((lanes >= low) & (lanes < low + width))
    return jnp.where(of_west, west, turn(east, width))


def own_halo(strips, a, b, rr):
    return halo_tile(strips[2, a:b], H * rr, strips[3, a:b], H * rr)


def corner_halo(strips, a, b, rr):
    slot, at = (5, H * (rr + ROWS)) if rr < H else (6, H * (rr - ROWS))
    slab = strips[slot, a:b]
    return halo_tile(slab, at, slab, at + H * H)


def row_valid(rr):
    n_lat = lax.axis_size("lat")
    row = lax.axis_index("lat") * ROWS + rr - H
    return jnp.where((row >= 0) & (row < ROWS * n_lat), 1.0, 0.0).astype(F32)


def wind_rows(wext, rr, step):
    zonal = wext[rr, 2 * step : 2 * step + 1, :]
    merid = wext[rr, 2 * step + 1 : 2 * step + 2, :]
    return zonal, merid, jnp.abs(zonal), jnp.abs(merid)


def spread(w):
    return jnp.broadcast_to(w, (8, RING))


def forward_row(src, wext, rr, step, emit):
    zonal, merid, az, am = wind_rows(wext, rr, step)
    valid = row_valid(rr)
    wc = spread((1.0 - az - am) * valid)
    wz = spread(az * valid)
    wm = spread(am * valid)
    from_east = spread(zonal) < 0
    from_north = spread(merid) < 0

    def part(c):
        here = src[rr, c : c + 8, :]
        along = jnp.where(from_east, pltpu.roll(here, RING - 1, 1), pltpu.roll(here, 1, 1))
        across = jnp.where(from_north, src[rr + 1, c : c + 8, :], src[rr - 1, c : c + 8, :])
        return wc * here + wz * along + wm * across

    for c in range(0, CH, 16):
        emit(c, part(c), part(c + 8))


def adjoint_row(src, wext, rr, step, emit):
    zonal, _, az, am = wind_rows(wext, rr, step)
    half = 0.5 * row_valid(rr)
    wc = spread((1.0 - az - am) * row_valid(rr))
    we = pltpu.roll(spread(half * (az - zonal)), 1, 1)
    ww = pltpu.roll(spread(half * (az + zonal)), RING - 1, 1)
    _, merid, _, am = wind_rows(wext, rr - 1, step)
    wn = spread(0.5 * row_valid(rr - 1) * (am - merid))
    _, merid, _, am = wind_rows(wext, rr + 1, step)
    ws = spread(0.5 * row_valid(rr + 1) * (am + merid))

    def part(c):
        here = src[rr, c : c + 8, :]
        return (
            wc * here
            + we * pltpu.roll(here, 1, 1)
            + ww * pltpu.roll(here, RING - 1, 1)
            + wn * src[rr - 1, c : c + 8, :]
            + ws * src[rr + 1, c : c + 8, :]
        )

    for c in range(0, CH, 16):
        emit(c, part(c), part(c + 8))


def advance(row, src, dst, wext, step, turns, per, base, emit=None):
    def store(rr):
        def put(c, low, high):
            dst[rr, c : c + 8, :] = low
            dst[rr, c + 8 : c + 16, :] = high

        return put

    def body(t, carry):
        for k in range(per):
            rr = base(t) + k
            row(src, wext, rr, step, (emit or store)(rr))
        return carry

    lax.fori_loop(0, turns, body, 0)


def inner(row, xa, xb, wext, steps, emit):
    src, dst = xa, xb
    for n in range(STEPS):
        first = H + 1 + n
        last = emit if n == STEPS - 1 else None
        count = ROWS - 2 - 2 * n
        per = 4 if count % 4 == 0 else 2
        advance(
            row, src, dst, wext, steps[n], count // per, per,
            lambda t, first=first, per=per: first + per * t, last,
        )
        src, dst = dst, src


def outer(row, xa, xb, wext, steps, emit):
    src, dst = xa, xb
    for n in range(STEPS):
        low, high = 1 + n, H + ROWS - 1 - n
        last = emit if n == STEPS - 1 else None
        advance(
            row, src, dst, wext, steps[n], 2, 4,
            lambda t, low=low, high=high: low + t * (high - low), last,
        )
        src, dst = dst, src


def cov_pair(base, ext, pat, lhs, cov, adjoint):
    for n in range(2):
        for b in range(2):
            m = (2 * n + b) * CH
            for k in range(OFFS):
                at = base + n + (2 * R - k if adjoint else k)
                at_pat = at if adjoint else base + n
                mask = pat[at_pat, 2 * k + b : 2 * k + b + 1, :]
                mask = jnp.broadcast_to(mask, (16, BLOCK)).astype(BF16)
                rows = ext[at, :, b * BLOCK : (b + 1) * BLOCK].reshape(CH // 16, 16, BLOCK)
                lhs[m : m + CH, k * BLOCK : (k + 1) * BLOCK] = (rows * mask[None]).reshape(CH, BLOCK)
    return jnp.dot(lhs[...], cov[...], preferred_element_type=F32)


def send_pair(ext, sems, index, up, down):
    return (
        send(ext.at[pl.ds(R + up, 2)], ext.at[pl.ds(R + up - ROWS, 2)], sems, index, NORTH),
        send(ext.at[pl.ds(R + down, 2)], ext.at[pl.ds(R + down + ROWS, 2)], sems, index + 1, SOUTH),
    )


def send_rows(field, stage, sems, index, up, down, count, at):
    here = pl.ds(at, count)
    stage[0, at : at + count] = field[H + up : H + up + count, :, 0:COLS].astype(BF16)
    north = send(stage.at[0, here], stage.at[2, here], sems, index, NORTH)
    stage[1, at : at + count] = field[H + down : H + down + count, :, 0:COLS].astype(BF16)
    south = send(stage.at[1, here], stage.at[3, here], sems, index + 1, SOUTH)
    return north, south


def place_rows(field, stage, north_order, south_order):
    low, high = row_valid(0), row_valid(EXT - 1)
    for k in range(H):
        field[k, :, 0:COLS] = stage[2, north_order[k]].astype(F32) * low
        field[ROWS + H + k, :, 0:COLS] = stage[3, south_order[k]].astype(F32) * high


def send_strips(strips, sems, index, put):
    put(0, COLS - LANES, LANES - H)
    east = send(strips.at[0], strips.at[2], sems, index, EAST)
    put(1, 0, 0)
    west = send(strips.at[1], strips.at[3], sems, index + 1, WEST)
    return east, west


def send_corners(strips, sems, index):
    strips[4] = corners(strips[2], strips[3])
    return (
        send(strips.at[4], strips.at[5], sems, index, NORTH),
        send(strips.at[4], strips.at[6], sems, index + 1, SOUTH),
    )


def pattern_table(pattern, table):
    table[...] = jnp.zeros_like(table)
    for k in range(OFFS):
        table[2 * k : 2 * k + 2, 0:ROWS] = pattern[k].astype(F32)
    shape = table.shape
    offset = lax.broadcasted_iota(jnp.int32, shape, 0) // 2 - R
    row = lax.axis_index("lat") * ROWS + lane_iota(shape) + offset
    inside = (row >= 0) & (row < ROWS * lax.axis_size("lat"))
    table[...] = jnp.where(inside, table[...], 0.0)


def records(jac, value, weight, column, count, wide, packed):
    slots = value.shape[0]
    live = lax.broadcasted_iota(jnp.int32, value.shape, 0) < jnp.broadcast_to(count[...], value.shape)
    cell = column[...]
    extra = (
        value[...].astype(F32),
        jnp.where(live, weight[...].astype(F32), 0.0),
        lax.shift_right_logical(cell, 8).astype(F32),
        jnp.bitwise_and(cell, COLS - 1).astype(F32),
    )

    def put(s, low):
        block = jnp.concatenate([jac[s].astype(F32), low], axis=0)
        wide[pl.ds(s, LANES, stride=slots), :] = block.T

    for s in range(4):
        put(s, extra[s])

    def rest(s, carry):
        put(s, jnp.zeros(value.shape, F32))
        return carry

    lax.fori_loop(4, slots, rest, 0)

    def narrow(t, carry):
        at = pl.multiple_of(t * 512, 512)
        packed[pl.ds(at, 512), :] = wide[pl.ds(at, 512), :].astype(BF16)
        return carry

    lax.fori_loop(0, SLOTS // 512, narrow, 0)


def record_copy(packed, rec, sems, other):
    per = SLOTS // peer_count()
    return pltpu.make_async_remote_copy(
        src_ref=packed.at[pl.ds(pl.multiple_of(other * per, per), per)],
        dst_ref=rec.at[pl.ds(pl.multiple_of(own_number() * per, per), per)],
        send_sem=sems.at[0],
        recv_sem=sems.at[1],
        device_id=other,
        device_id_type=pl.DeviceIdType.LOGICAL,
    )


def send_records(packed, rec, sems, first, last):
    for_peers(first, last, lambda other: record_copy(packed, rec, sems, other).start())


def wait_records(packed, rec, sems):
    most = pl.ds(0, SLOTS - SLOTS // peer_count())
    both = pltpu.make_async_remote_copy(
        src_ref=packed.at[most],
        dst_ref=rec.at[most],
        send_sem=sems.at[0],
        recv_sem=sems.at[1],
        device_id=neighbours()[0],
        device_id_type=MESH,
    )
    both.wait_send()
    both.wait_recv()


def forward_kernel(
    ctrl, winds, pattern, cov, jac, value, weight, column, count, fin, wout, pout, rec,
    raw, ext, tables, pf, lhs, covcat, xa, xb, stage, wext, strips, wide_rec, packed, sems, local, rsems,
):
    order = (14, 15, 0, 1, 12, 13, 2, 3, 10, 11, 4, 5, 6, 7, 8, 9)
    rows_in = {r: pltpu.make_async_copy(ctrl.at[:, r, :], raw.at[r], local.at[0, r]) for r in order}
    winds_in = [
        pltpu.make_async_copy(winds.at[:, r, :], wext.at[H + r, :, pl.ds(0, COLS)], local.at[1, r])
        for r in range(ROWS)
    ]
    for r in order:
        rows_in[r].start()
    for copy in winds_in:
        copy.start()
    greet_all()
    pattern_table(pattern, tables.at[0])
    for r in order:
        rows_in[r].wait()
        ext[R + r] = raw[r].astype(BF16)
    for k in range(OFFS):
        covcat[k * BLOCK : (k + 1) * BLOCK, :] = cov[abs(k - R)]
    for r in range(ROWS):
        pf[r] = jnp.broadcast_to(tables[0, :, r : r + 1], (32, BLOCK))
    wait(winds_in)
    greeted(peer_count() - 1)
    chunks = [
        send_pair(ext, sems, 2 * n, up, down)
        for n, (up, down) in enumerate(((14, 0), (12, 2), (10, 4)))
    ]
    wide = pl.ds(0, COLS)
    wind_rows_sent = (
        send(wext.at[pl.ds(ROWS, H), :, wide], wext.at[pl.ds(0, H), :, wide], sems, 6, NORTH),
        send(wext.at[pl.ds(H, H), :, wide], wext.at[pl.ds(ROWS + H, H), :, wide], sems, 7, SOUTH),
    )
    patterns = [
        send(tables.at[0], tables.at[1], sems, 16, NORTH),
        send(tables.at[0], tables.at[2], sems, 17, SOUTH),
    ]
    records(jac, value, weight, column, count, wide_rec, packed)
    per = SLOTS // peer_count()
    mine = pl.ds(pl.multiple_of(own_number() * per, per), per)
    own = pltpu.make_async_copy(packed.at[mine], rec.at[mine], local.at[2, 0])
    own.start()

    def pairs(first, gap):
        for t in range(2):
            base = first + gap * t
            y = cov_pair(base, ext, pf, lhs.at[t], covcat, False)
            for n in range(2):
                for b in range(2):
                    m = (2 * n + b) * CH
                    xa[H + base + n, :, b * BLOCK : (b + 1) * BLOCK] = y[m : m + CH]

    pairs(6, 2)
    wait(chunks[0])
    pairs(4, 6)
    wait(chunks[1])
    pairs(2, 10)
    near = send_rows(xa, stage, sems, 8, 12, 2, 2, 0)
    wait(chunks[2])
    pairs(0, 14)
    far = send_rows(xa, stage, sems, 10, 14, 0, 2, 2)

    def put(slot, at, first):
        strips[slot, 0:CH] = pack_strip(lambda rr: xa[rr, :, at : at + LANES], first)
        strips[slot, CH : CH + 8] = pack_strip(lambda rr: wext[rr, :, at : at + LANES], first)

    wait(send_strips(strips, sems, 12, put))
    turned = send_corners(strips, sems, 14)
    send_records(packed, rec, rsems, 1, peer_count())
    for rr in range(H, H + ROWS):
        xa[rr, :, COLS:RING] = own_halo(strips, 0, CH, rr)
        wext[rr, :, COLS:RING] = own_halo(strips, CH, CH + 8, rr)

    def emit(rr):
        def put(c, low, high):
            raw[rr - H, c : c + 8, :] = low[:, 0:COLS]
            raw[rr - H, c + 8 : c + 16, :] = high[:, 0:COLS]

        return put

    def put_out(first, count, index):
        here = pl.ds(first, count)
        copy = pltpu.make_async_copy(raw.at[here], fin.at[here], local.at[2, index])
        copy.start()
        return copy

    steps = tuple(range(STEPS))
    inner(forward_row, xa, xb, wext, steps, emit)
    outgoing = [put_out(4, 8, 1)]
    wait(near + far + turned + wind_rows_sent)
    place_rows(xa, stage, (0, 1, 2, 3), (2, 3, 0, 1))
    for rr in (*range(H), *range(H + ROWS, EXT)):
        xa[rr, :, COLS:RING] = corner_halo(strips, 0, CH, rr) * row_valid(rr)
        wext[rr, :, COLS:RING] = corner_halo(strips, CH, CH + 8, rr)
    outer(forward_row, xa, xb, wext, steps, emit)
    outgoing += [put_out(0, 4, 2), put_out(12, 4, 3)]
    wout[...] = wext[...]
    wait(patterns)
    pout[...] = tables[...]
    own.wait()
    wait(outgoing)
    wait_records(packed, rec, rsems)


def adjoint_kernel(
    forcing, winds, pattern, cov, ctrl, out,
    ext, pf, lhs, covcat, xa, xb, stage, strips, back, sems, local,
):
    incoming = [
        pltpu.make_async_copy(ctrl.at[:, r, :], back.at[r], local.at[1, r]) for r in range(ROWS)
    ]
    greet()
    fields = [
        pltpu.make_async_copy(
            forcing.at[pl.ds(first, count)],
            xa.at[pl.ds(H + first, count), :, pl.ds(0, COLS)],
            local.at[2, first],
        )
        for first, count in ((12, 4), (0, 4), (4, 8))
    ]
    for copy in fields + incoming:
        copy.start()
    wait(fields)
    strips[0] = pack_strip(lambda rr: xa[rr, :, COLS - LANES : COLS], LANES - H)
    strips[1] = pack_strip(lambda rr: xa[rr, :, 0:LANES], 0)
    greeted(4)
    sides = (
        send(strips.at[0], strips.at[2], sems, 2, EAST),
        send(strips.at[1], strips.at[3], sems, 3, WEST),
    )
    rows = send_rows(xa, stage, sems, 0, 12, 0, 4, 0)
    for k in range(R + 1):
        turned = cov[k].astype(F32).T.astype(BF16)
        for at in {R + k, R - k}:
            covcat[at * BLOCK : (at + 1) * BLOCK, :] = turned
    for i in range(WIDE):
        r = i - R
        slot, lane = (1, r + ROWS) if r < 0 else (2, r - ROWS) if r >= ROWS else (0, r)
        pf[i] = jnp.broadcast_to(pattern[slot, :, lane : lane + 1], (32, BLOCK))
    wait(sides)
    turned = send_corners(strips, sems, 4)
    for rr in range(H, H + ROWS):
        xa[rr, :, COLS:RING] = own_halo(strips, 0, CH, rr)

    def emit(rr):
        def put(c, low, high):
            both = jnp.concatenate([low[:, 0:COLS], high[:, 0:COLS]], axis=0)
            ext[rr - H + R, c : c + 16, :] = both.astype(BF16)

        return put

    steps = tuple(range(STEPS - 1, -1, -1))
    inner(adjoint_row, xa, xb, winds, steps, emit)
    chunks = [send_pair(ext, sems, 6, 10, 4)]
    wait(rows + turned)
    place_rows(xa, stage, (0, 1, 2, 3), (0, 1, 2, 3))
    for rr in (*range(H), *range(H + ROWS, EXT)):
        xa[rr, :, COLS:RING] = corner_halo(strips, 0, CH, rr)
    outer(adjoint_row, xa, xb, winds, steps, emit)
    chunks.append(send_pair(ext, sems, 8, 14, 0))
    chunks.append(send_pair(ext, sems, 10, 12, 2))
    outgoing = []
    wait(incoming)

    def pairs(first, gap):
        for t in range(2):
            base = first + gap * t
            y = cov_pair(base, ext, pf, lhs.at[t], covcat, True)
            for n in range(2):
                for b in range(2):
                    m = (2 * n + b) * CH
                    lanes = slice(b * BLOCK, (b + 1) * BLOCK)
                    back[base + n, :, lanes] = back[base + n, :, lanes] + y[m : m + CH]
        for r in (first, first + 1, first + gap, first + gap + 1):
            copy = pltpu.make_async_copy(back.at[r], out.at[:, r, :], local.at[0, r])
            copy.start()
            outgoing.append(copy)

    pairs(6, 2)
    wait(chunks[1])
    pairs(4, 6)
    wait(chunks[2])
    pairs(2, 10)
    wait(chunks[0])
    pairs(0, 14)
    wait(outgoing)


def obs_kernel(rec, fin, forcing, forecast, field, f2, r32, aux, ct, rowb, yt, zt, local):
    per = 32
    field_in = pltpu.make_async_copy(fin, field, local.at[ROWS])
    field_in.start()

    def widen(t, carry):
        at = pl.multiple_of(t * 512, 512)
        r32[pl.ds(at, 512), :] = rec[pl.ds(at, 512), :].astype(F32)
        return carry

    lax.fori_loop(0, SLOTS // 512, widen, 0)
    group = lane_iota((per, LANES)) // per
    for k in range(4):
        total = jnp.zeros((per, LANES), F32)
        for q in range(4):
            part = r32[pl.ds(q * per + k, per, stride=4 * per), :]
            total = jnp.where(group == q, turn(part, per * q + per), total)
        aux[k] = total
    field_in.wait()
    outgoing = []
    for r in range(ROWS):
        copy = pltpu.make_async_copy(field.at[r], forecast.at[:, r, :], local.at[r])
        copy.start()
        outgoing.append(copy)
    for r in range(ROWS):
        high = field[r].astype(BF16)
        f2[0, r * CH : (r + 1) * CH, :] = high
        f2[1, r * CH : (r + 1) * CH, :] = (field[r] - high.astype(F32)).astype(BF16)
    sub = lax.broadcasted_iota(jnp.int32, (COLS, TILE), 0).astype(F32)

    def vector(k, t):
        return jnp.concatenate([aux[k, pl.ds(2 * t, 1), :], aux[k, pl.ds(2 * t + 1, 1), :]], axis=1)

    def gather(t):
        at = pl.multiple_of(t * TILE, TILE)
        value, weight, row, col = (vector(k, t) for k in range(4))
        hot = jnp.where(jnp.broadcast_to(col, (COLS, TILE)) == sub, 1.0, 0.0).astype(BF16)
        ct[:, pl.ds(at, TILE)] = hot
        row8 = jnp.broadcast_to(row, (8, TILE))
        rowb[:, pl.ds(at, TILE)] = jnp.broadcast_to(row, (16, TILE)).astype(BF16)
        halves = []
        for part in range(2):
            got = jnp.zeros((CH // 8, 8, TILE), F32)
            for g in range(0, ROWS, GROUP):
                rows = f2[part, g * CH : (g + GROUP) * CH, :]
                some = jnp.dot(rows, hot, preferred_element_type=F32)
                for k in range(GROUP):
                    piece = some[k * CH : (k + 1) * CH].reshape(CH // 8, 8, TILE)
                    got = jnp.where((row8 == float(g + k))[None], piece, got)
            halves.append(got)
        got = (halves[0] + halves[1]).reshape(CH, TILE)
        jac = jnp.concatenate(
            [r32[pl.ds(at, LANES), :].T[0:CH], r32[pl.ds(at + LANES, LANES), :].T[0:CH]], axis=1
        )
        evolved = jnp.sum(jac * got, axis=0, keepdims=True)
        residual = weight * (evolved - value)
        yt[:, pl.ds(at, TILE)] = (jac * residual).astype(BF16)

    def four_tiles(t, carry):
        for n in range(4):
            gather(4 * t + n)
        return carry

    lax.fori_loop(0, SLOTS // TILE // 4, four_tiles, 0)
    wait(outgoing)

    def scatter(g, zt):
        for k in range(GROUP):
            want = float(g * GROUP + k)
            for c in range(0, SLOTS, 512):
                here = jnp.where(rowb[:, c : c + 512].astype(F32) == want, 1.0, 0.0).astype(BF16)
                part = yt[:, c : c + 512].reshape(CH // 16, 16, 512) * here[None]
                zt[k * CH : (k + 1) * CH, c : c + 512] = part.reshape(CH, 512)
        total = lax.dot_general(
            zt[...], ct[...], (((1,), (1,)), ((), ())), preferred_element_type=F32
        )
        for k in range(GROUP):
            field[g * GROUP + k] = total[k * CH : (k + 1) * CH]
        put_out(g).start()

    def put_out(g):
        here = pl.ds(g * GROUP, GROUP)
        return pltpu.make_async_copy(field.at[here], forcing.at[here], local.at[g])

    for g in range(ROWS // GROUP):
        scatter(g, zt.at[g % 2])
    wait([put_out(g) for g in range(ROWS // GROUP)])


def vmem(n):
    return [pl.BlockSpec(memory_space=pltpu.VMEM)] * n


def anywhere(n):
    return [pl.BlockSpec(memory_space=pl.ANY)] * n


def params(**more):
    return pltpu.CompilerParams(vmem_limit_bytes=60 * 1024 * 1024, **more)


def advection_scratch(strip_rows):
    return [
        pltpu.VMEM((EXT, CH, RING), F32),
        pltpu.VMEM((EXT, CH, RING), F32),
        pltpu.VMEM((4, H, CH, COLS), BF16),
        pltpu.VMEM((7, strip_rows, LANES), F32),
    ]


def covariance_scratch(pattern_rows):
    return [
        pltpu.VMEM((pattern_rows, 32, BLOCK), F32),
        pltpu.VMEM((2, 4 * CH, OFFS * BLOCK), BF16),
        pltpu.VMEM((OFFS * BLOCK, BLOCK), BF16),
    ]


def forward_call(*args):
    xa, xb, stage, strips = advection_scratch(CH + 8)
    return pl.pallas_call(
        forward_kernel,
        name="forward",
        out_shape=(
            jax.ShapeDtypeStruct((ROWS, CH, COLS), F32),
            jax.ShapeDtypeStruct((EXT, 8, RING), F32),
            jax.ShapeDtypeStruct((3, 32, LANES), F32),
            jax.ShapeDtypeStruct((SLOTS, LANES), BF16),
        ),
        in_specs=anywhere(2) + vmem(7),
        out_specs=tuple(anywhere(1) + vmem(2) + anywhere(1)),
        scratch_shapes=[
            pltpu.VMEM((ROWS, CH, COLS), F32),
            pltpu.VMEM((WIDE, CH, COLS), BF16),
            pltpu.VMEM((3, 32, LANES), F32),
            *covariance_scratch(ROWS),
            xa,
            xb,
            stage,
            pltpu.VMEM((EXT, 8, RING), F32),
            strips,
            pltpu.VMEM((SLOTS, LANES), F32),
            pltpu.VMEM((SLOTS, LANES), BF16),
            pltpu.SemaphoreType.DMA((2, 18)),
            pltpu.SemaphoreType.DMA((3, ROWS)),
            pltpu.SemaphoreType.DMA((2,)),
        ],
        compiler_params=params(collective_id=0, has_side_effects=True),
        cost_estimate=pl.CostEstimate(
            flops=3_000_000_000, bytes_accessed=16_000_000, transcendentals=0
        ),
    )(*args)


def adjoint_call(forcing, winds, pattern, cov, ctrl):
    xa, xb, stage, strips = advection_scratch(CH)
    return pl.pallas_call(
        adjoint_kernel,
        name="adjoint",
        out_shape=jax.ShapeDtypeStruct((CH, ROWS, COLS), F32),
        in_specs=anywhere(1) + vmem(3) + anywhere(1),
        out_specs=anywhere(1)[0],
        scratch_shapes=[
            pltpu.VMEM((WIDE, CH, COLS), BF16),
            *covariance_scratch(WIDE),
            xa,
            xb,
            stage,
            strips,
            pltpu.VMEM((ROWS, CH, COLS), F32),
            pltpu.SemaphoreType.DMA((2, 12)),
            pltpu.SemaphoreType.DMA((3, ROWS)),
        ],
        compiler_params=params(collective_id=1, has_side_effects=True),
    )(forcing, winds, pattern, cov, ctrl)


PIECES = 8


def copy_kernel(field, out, held, sems):
    share = CH // PIECES
    pieces = [pl.ds(n * share, share) for n in range(PIECES)]
    inward = [own_copy(field.at[p], held.at[p], sems.at[0, n]) for n, p in enumerate(pieces)]
    outward = []
    for n, p in enumerate(pieces):
        inward[n].wait()
        outward.append(own_copy(held.at[p], out.at[p], sems.at[1, n]))
    wait(outward)


def own_copy(src, dst, sem):
    copy = pltpu.make_async_copy(src, dst, sem)
    copy.start()
    return copy


def copy_call(field):
    return pl.pallas_call(
        copy_kernel,
        name="copy_out",
        out_shape=jax.ShapeDtypeStruct((CH, ROWS, COLS), F32),
        in_specs=anywhere(1),
        out_specs=anywhere(1)[0],
        scratch_shapes=[pltpu.VMEM((CH, ROWS, COLS), F32), pltpu.SemaphoreType.DMA((2, PIECES))],
        compiler_params=params(),
    )(field)


def obs_call(rec, fin):
    return pl.pallas_call(
        obs_kernel,
        name="observe",
        out_shape=(
            jax.ShapeDtypeStruct((ROWS, CH, COLS), F32),
            jax.ShapeDtypeStruct((CH, ROWS, COLS), F32),
        ),
        in_specs=vmem(1) + anywhere(1),
        out_specs=tuple(anywhere(2)),
        scratch_shapes=[
            pltpu.VMEM((ROWS, CH, COLS), F32),
            pltpu.VMEM((2, ROWS * CH, COLS), BF16),
            pltpu.VMEM((SLOTS, LANES), F32),
            pltpu.VMEM((4, 32, LANES), F32),
            pltpu.VMEM((COLS, SLOTS), BF16),
            pltpu.VMEM((16, SLOTS), BF16),
            pltpu.VMEM((CH, SLOTS), BF16),
            pltpu.VMEM((2, GROUP * CH, SLOTS), BF16),
            pltpu.SemaphoreType.DMA((ROWS + 1,)),
        ],
        compiler_params=params(),
    )(rec, fin)


def on_device(
    control, winds, pattern, cov_tables, jacobians, obs_value, obs_weight, obs_column, obs_count
):
    wind2 = winds.reshape(2 * STEPS, ROWS, COLS)
    fin, wext, table, rec = forward_call(
        control,
        wind2,
        jnp.transpose(pattern, (2, 1, 0)),
        cov_tables,
        jnp.transpose(jacobians[0], (1, 2, 0)),
        obs_value[0].T,
        obs_weight[0].T,
        obs_column[0].T,
        obs_count,
    )
    forcing, forecast = obs_call(rec, fin)
    gradient = adjoint_call(forcing, wext, table, cov_tables, control)
    return forecast, copy_call(gradient)


def solution(mesh):
    in_specs = (
        P(None, "lat", "lon"),
        P(None, None, "lat", "lon"),
        P("lat", "lon", None),
        P(),
        P(("lat", "lon"), None, None, None),
        P(("lat", "lon"), None, None),
        P(("lat", "lon"), None, None),
        P(("lat", "lon"), None, None),
        P(("lat", "lon"), None),
    )
    out_specs = (P(None, "lat", "lon"), P(None, "lat", "lon"))
    return jax.shard_map(
        on_device, mesh=mesh, in_specs=in_specs, out_specs=out_specs, check_vma=False
    )
```
